32 devices in a mesh: dp: 4 (over y, x), expert: 8 (over z, core).
Axes of the slice: x: 2, y: 2, z: 4, core: 2. Of those that a mesh axis runs over, the one named last changes fastest.
Arguments:
- tokens: bfloat16 [4096, 2048], P(('dp', 'expert')), may hold values from -6 to 6
- out_grad: bfloat16 [4096, 2048], P(('dp', 'expert')), may hold values from -6 to 6
- routes: int32 [4096, 3], P(('dp', 'expert')), may hold values from 0 to 7, all different within a row; in each aligned block of 128 rows (0 to 127, 128 to 255, ...) at most 64 rows name the same one
- probs: bfloat16 [4096, 3], P(('dp', 'expert')), may hold values from 0.099609375 to 1
- w_in: bfloat16 [8, 2048, 1536], P('expert'), may hold values from -0.125 to 0.125
- w_out: bfloat16 [8, 768, 2048], P('expert'), may hold values from -0.21875 to 0.21875
Outputs:
- token_grad: bfloat16 [4096, 2048], P(('dp', 'expert'))
- prob_grad: bfloat16 [4096, 3], P(('dp', 'expert'))
- w_in_grad: bfloat16 [8, 2048, 1536], P('expert', 'dp')
- w_out_grad: bfloat16 [8, 768, 2048], P('expert', None, 'dp')
The draws below stay inside these ranges and needn't reach their ends.
Inputs may be any that keep to these rules, and one draw needn't show every extreme that they name: `routes`: each row names 3 different experts. In each device's aligned block of 128 rows no expert is named more than 64 times, a bound that some block reaches.
All inputs are finite; a program needn't handle non-finite values.
Results may differ from the reference program's by a relative error of at most 0.014.
Values may be sent and summed in bfloat16 or wider, within the bound.
A program may use at most 128 MiB of HBM per device.

```python
import math
import jax
import jax.numpy as jnp
import numpy as np
from jax import lax

D = 2048
F = 768
TOP = 3
TOK_DEV = 128
EXPERTS = 8
CAP = 64
TOKENS = 4096


def levels(own_key, shape, shards, least, high):
    level, own = 1.0, jax.random.fold_in(own_key, 6)
    for position, blocks in shards:
        draws = jnp.exp(jax.random.uniform(jax.random.fold_in(own, position), (blocks,), jnp.float32, least / len(shards), high / len(shards)))
        level = level * jnp.repeat(draws, shape[position] // blocks).reshape([-1 if axis == position else 1 for axis in range(len(shape))])
    return level


def deal_out(stream_key, own, number, rows, amount, top, limit, skew):
    order = jax.random.permutation(stream_key, amount)
    packed, usual = shares(amount, rows * top, limit, skew, True), shares(amount, rows * top, limit, skew, False)
    places = jnp.arange(amount)

    def named(tallies, offset_by):
        used = int((tallies > 0).sum())
        fixed = max(1, used // 4)
        shifted = fixed + (places - fixed + offset_by * (used - fixed)) % max(1, amount - fixed)
        return jnp.zeros((amount,), jnp.int32).at[order[jnp.where(places < fixed, places, shifted)]].set(jnp.asarray(tallies, jnp.int32))

    tallies = jnp.where(number % 4 == 0, named(packed, number // 4), named(usual, number - number // 4 - 1))
    mixed = jax.random.permutation(jax.random.fold_in(own, 3), amount)
    source_of, receiver = mixed[0:amount // 2 * 2:2], mixed[1:amount // 2 * 2:2]
    margin = jnp.minimum(tallies[source_of] - 1, limit - tallies[receiver]) // 2
    margin = jnp.where((source_of == order[0]) | (receiver == order[0]) | (tallies[receiver] == 0), 0, jnp.maximum(margin, 0))
    shifted = jax.random.randint(jax.random.fold_in(own, 4), (amount // 2,), 0, 1 << 20) % (margin + 1)
    tallies = tallies.at[source_of].add(-shifted).at[receiver].add(shifted)
    members = jnp.searchsorted(jnp.cumsum(tallies), jnp.arange(rows * top), side="right").astype(jnp.int32)
    listing = members.reshape(top, rows).T
    listing = listing[jax.random.permutation(jax.random.fold_in(own, 1), rows)]
    offset_by = jax.random.randint(jax.random.fold_in(own, 2), (rows, 1), 0, top)
    return jnp.take_along_axis(listing, (jnp.arange(top)[None, :] + offset_by) % top, axis=1)


def shares(count, total, most, skew, full):
    loads = [(1 << 20) // math.isqrt(standing ** skew) + 1 for standing in range(1, count + 1)]
    largest = most if full else min(most, max(-(-total // count), total * loads[0] // sum(loads)))
    least = 1 if total - largest >= count - 1 else 0
    holding, spare = [largest] + [least] * (count - 1), total - largest - least * (count - 1)
    while spare > 0:
        movable = [i for i in range(1, count) if holding[i] < largest] or [i for i in range(1, count) if holding[i] < most]
        whole, remaining = sum([loads[i] for i in movable]), spare
        for i in movable:
            extra = min(most - holding[i], max(1, remaining * loads[i] // whole), spare)
            holding[i] = holding[i] + extra
            spare = spare - extra
    return np.array(holding)


def noise(stream_key, shape, spread, limit, pieces=(), kind=jnp.bfloat16):
    gain = levels(stream_key, shape, pieces, -0.22, 0.18) if pieces else 1.0
    entries = jax.random.normal(stream_key, shape, jnp.float32) * spread * gain
    return jnp.minimum(jnp.maximum(entries, -limit), limit).astype(kind)


def setup_inputs(seed: int = 0) -> dict:
    seeds = jax.random.split(jax.random.key(seed), 7)
    tokens = noise(seeds[0], (TOKENS, D), 1.0, 6.0, ((0, 32),))
    out_grad = noise(seeds[1], (TOKENS, D), 1.0, 6.0, ((0, 32),))
    routes_keys = jax.random.split(jax.random.fold_in(seeds[2], 1), TOKENS // TOK_DEV)
    routes_turns = jax.random.permutation(jax.random.fold_in(seeds[2], 3), TOKENS // TOK_DEV)
    routes = jax.vmap(lambda own, number: deal_out(jax.random.fold_in(seeds[2], 2), own, number, TOK_DEV, EXPERTS, TOP, CAP, 2))(routes_keys, routes_turns).reshape((TOKENS, TOP))
    probs = jnp.clip(jnp.exp(math.log(1.0) - 2.306499 * jax.random.uniform(seeds[3], (TOKENS, TOP), jnp.float32) ** levels(seeds[3], (TOKENS, TOP), ((0, 32),), -0.2, 0.2)), 0.099609375, 1.0).astype(jnp.bfloat16)
    w_in = noise(seeds[4], (EXPERTS, D, 2 * F), D ** -0.5, 0.125, ((0, 8),))
    w_out = noise(seeds[5], (EXPERTS, F, D), F ** -0.5, 0.21875, ((0, 8),))
    return {"tokens": tokens, "out_grad": out_grad, "routes": routes, "probs": probs, "w_in": w_in, "w_out": w_out}


def silu_parts(gate):
    sig = jax.nn.sigmoid(gate)
    return gate * sig, sig * (1.0 + gate * (1.0 - sig))


def reference(tokens, out_grad, routes, probs, w_in, w_out):
    flat = routes.reshape(-1).astype(jnp.int32)
    maxrows = CAP * (TOKENS // TOK_DEV)
    order = jnp.argsort(flat, stable=True).astype(jnp.int32)
    counts = jnp.sum((flat[:, None] == jnp.arange(EXPERTS, dtype=jnp.int32)[None, :]).astype(jnp.int32), axis=0)
    offsets = (jnp.cumsum(counts) - counts).astype(jnp.int32)
    padded = jnp.concatenate([order, jnp.zeros((maxrows,), jnp.int32)])
    probs_flat = probs.reshape(-1)

    def per_expert(carry, inputs):
        grad_acc, prob_acc = carry
        w_one, w_two, offset, total = inputs
        index = lax.dynamic_slice(padded, (offset.astype(jnp.int32),), (maxrows,))
        valid = jnp.arange(maxrows, dtype=jnp.int32) < total
        source = index // TOP
        rows_x = jnp.where(valid[:, None], tokens[source], jnp.zeros((), tokens.dtype))
        rows_dy = jnp.where(valid[:, None], out_grad[source], jnp.zeros((), out_grad.dtype))
        rows_p = jnp.where(valid, probs_flat[index], jnp.zeros((), probs.dtype))
        proj = jnp.dot(rows_x, w_one, preferred_element_type=jnp.float32)
        gate, upper = proj[:, :F], proj[:, F:]
        act, slope = silu_parts(gate)
        hid = (act * upper).astype(jnp.bfloat16)
        outs = jnp.dot(hid, w_two, preferred_element_type=jnp.float32).astype(jnp.bfloat16)
        dprob = jnp.sum(rows_dy.astype(jnp.float32) * outs.astype(jnp.float32), axis=1).astype(jnp.bfloat16)
        slot_grad = (rows_p.astype(jnp.float32)[:, None] * rows_dy.astype(jnp.float32)).astype(jnp.bfloat16)
        hid_grad = jnp.dot(slot_grad, w_two.T, preferred_element_type=jnp.float32)
        proj_grad = jnp.concatenate([hid_grad * upper * slope, hid_grad * act], axis=1).astype(jnp.bfloat16)
        row_grad = jnp.dot(proj_grad, w_one.T, preferred_element_type=jnp.float32).astype(jnp.bfloat16)
        grad_one = lax.dot_general(rows_x, proj_grad, (((0,), (0,)), ((), ())), preferred_element_type=jnp.float32)
        grad_two = lax.dot_general(hid, slot_grad, (((0,), (0,)), ((), ())), preferred_element_type=jnp.float32)
        grad_acc = grad_acc.at[source].add(jnp.where(valid[:, None], row_grad.astype(jnp.float32), jnp.float32(0.0)))
        prob_acc = prob_acc.at[index].add(jnp.where(valid, dprob.astype(jnp.float32), jnp.float32(0.0)))
        return (grad_acc, prob_acc), (grad_one.astype(jnp.bfloat16), grad_two.astype(jnp.bfloat16))

    start = (jnp.zeros((TOKENS, D), jnp.float32), jnp.zeros((TOKENS * TOP,), jnp.float32))
    (grad_acc, prob_acc), (w_in_grad, w_out_grad) = lax.scan(per_expert, start, (w_in, w_out, offsets, counts))
    return (grad_acc.astype(jnp.bfloat16), prob_acc.reshape(TOKENS, TOP).astype(jnp.bfloat16), w_in_grad, w_out_grad)
```

```python
import jax
import jax.numpy as jnp
from jax import lax
from jax.experimental import pallas as pl
from jax.experimental.pallas import tpu as pltpu
from jax.sharding import PartitionSpec as P

F32 = jnp.float32
BF16 = jnp.bfloat16


def gather_kernel(n, cap, top, *refs):
    count = 3
    ins, w_hbm = refs[:count], refs[count]
    table_out, rows_x, rows_dy, proj = refs[count + 1 : count + 5]
    all_x, all_dy, w_vmem, w_sem, own_sem, send_sem, recv_sem = refs[count + 5 :]
    outs = (table_out, all_x, all_dy)
    load_w = pltpu.make_async_copy(w_hbm, w_vmem, w_sem)
    load_w.start()
    chips = n // 2
    me = lax.axis_index("expert")
    z, core = me // 2, me % 2
    ways = (
        (me - core + 1 - core, None),
        (me + 2, z < chips - 1),
        (me - 2, z > 0),
    )

    def guarded(ok, body):
        if ok is None:
            body()
        else:
            pl.when(ok)(body)

    barrier = pltpu.get_barrier_semaphore()
    for target, ok in ways:
        guarded(ok, lambda target=target: pl.semaphore_signal(
            barrier, inc=1, device_id={"expert": target}, device_id_type=pl.DeviceIdType.MESH
        ))
    peers = 1 + (z < chips - 1).astype(jnp.int32) + (z > 0).astype(jnp.int32)
    pl.semaphore_wait(barrier, peers)

    def copy(a, slot, hop, way):
        source = ins[a] if hop is None else outs[a].at[slot]
        return pltpu.make_async_remote_copy(
            src_ref=source,
            dst_ref=outs[a].at[slot],
            send_sem=send_sem.at[a, 0 if hop is None else hop, way],
            recv_sem=recv_sem.at[a, slot],
            device_id={"expert": ways[way][0]},
            device_id_type=pl.DeviceIdType.MESH,
        )

    def locals_():
        return [pltpu.make_async_copy(ins[a], outs[a].at[me], own_sem.at[a]) for a in range(count)]

    for c in locals_():
        c.start()
    hops = []
    for step in range(1, chips):
        hops.append((2 * step - 1, me - 2 * step, z - step >= 0, 1))
        hops.append((2 * step, me + 2 * step, z + step < chips, 2))
    def pick(rows_in, rows_out):
        tok = rows_in.shape[1]
        earlier = (
            lax.broadcasted_iota(jnp.int32, (tok, tok), 0) < lax.broadcasted_iota(jnp.int32, (tok, tok), 1)
        )
        earlier = jnp.where(earlier, 1.0, 0.0).astype(BF16)
        order = lax.broadcasted_iota(jnp.int32, (cap, tok), 0).astype(F32)

        def one(b, carry):
            named = table_out[b].astype(F32)
            hit = jnp.zeros((1, tok), F32)
            for k in range(top):
                hit = hit + jnp.where(named[k : k + 1] == me.astype(F32), 1.0, 0.0)
            rank = jnp.dot(
                jnp.broadcast_to(hit, (16, tok)).astype(BF16), earlier, preferred_element_type=F32
            )[0:1]
            place = jnp.where(order == rank, 1.0, 0.0) * hit
            rows_out[pl.ds(pl.multiple_of(b * cap, cap), cap), :] = jnp.dot(
                place.astype(BF16), rows_in[b], preferred_element_type=F32
            ).astype(BF16)
            return carry

        lax.fori_loop(0, n, one, 0)

    def send_own(a):
        for way in (1, 2, 0):
            guarded(ways[way][1], lambda a=a, way=way: copy(a, me, None, way).start())

    def pass_on(a):
        for hop, slot, here, way in hops:

            def relay(a=a, hop=hop, slot=slot, way=way):
                copy(a, slot, hop, way).wait_recv()
                pl.when(ways[way][1])(lambda: copy(a, slot, hop, way).start())
                copy(a, slot, hop, 0).start()

            pl.when(here)(relay)

    def finish(a):
        for chip in range(chips):
            copy(a, 2 * chip + 1 - core, 0, 0).wait_recv()

    send_own(0)
    send_own(1)
    pass_on(0)
    pass_on(1)
    send_own(2)
    for c in locals_():
        c.wait()
    finish(0)
    finish(1)
    load_w.wait()
    tile = 256
    steps = proj.shape[1] // tile
    width = steps // len(hops) if steps >= len(hops) else 0

    def columns(first, last):
        def one(i, carry):
            at = pl.ds(pl.multiple_of(i * tile, tile), tile)
            proj[:, at] = jnp.dot(rows_x[...], w_vmem[:, at], preferred_element_type=F32)
            return carry

        lax.fori_loop(first, last, one, 0)

    pick(all_x, rows_x)
    for i, (hop, slot, here, way) in enumerate(hops):

        def relay(hop=hop, slot=slot, way=way):
            copy(2, slot, hop, way).wait_recv()
            pl.when(ways[way][1])(lambda: copy(2, slot, hop, way).start())
            copy(2, slot, hop, 0).start()

        pl.when(here)(relay)
        columns(i * width, (i + 1) * width if i < len(hops) - 1 else steps)
    finish(2)
    pick(all_dy, rows_dy)
    for a in range(count):
        for way in range(3):
            guarded(ways[way][1], lambda a=a, way=way: copy(a, me, None, way).wait_send())
        for hop, slot, here, way in hops:

            def drain(a=a, hop=hop, slot=slot, way=way):
                pl.when(ways[way][1])(lambda: copy(a, slot, hop, way).wait_send())
                copy(a, slot, hop, 0).wait_send()

            pl.when(here)(drain)


def gather_all(n, cap, top, w_one, *arrays):
    table, rows = arrays[:2]
    vmem, width = pl.BlockSpec(memory_space=pltpu.VMEM), rows.shape[1]
    return pl.pallas_call(
        lambda *refs: gather_kernel(n, cap, top, *refs),
        out_shape=[
            jax.ShapeDtypeStruct((n,) + table.shape, BF16),
            jax.ShapeDtypeStruct((n * cap, width), BF16),
            jax.ShapeDtypeStruct((n * cap, width), BF16),
            jax.ShapeDtypeStruct((n * cap, w_one.shape[1]), F32),
        ],
        in_specs=[vmem] * 3 + [pl.BlockSpec(memory_space=pl.ANY)],
        out_specs=[vmem] * 4,
        scratch_shapes=[
            pltpu.VMEM((n,) + rows.shape, BF16),
            pltpu.VMEM((n,) + rows.shape, BF16),
            pltpu.VMEM(w_one.shape, BF16),
            pltpu.SemaphoreType.DMA,
            pltpu.SemaphoreType.DMA((3,)),
            pltpu.SemaphoreType.DMA((3, n - 1, 3)),
            pltpu.SemaphoreType.DMA((3, n)),
        ],
        compiler_params=pltpu.CompilerParams(
            collective_id=0, has_side_effects=True, vmem_limit_bytes=48 * 1024 * 1024
        ),
    )(*arrays, w_one)


def exclusive_rank(hits):
    rows = hits.shape[1]
    earlier = (jnp.arange(rows)[:, None] < jnp.arange(rows)[None, :]).astype(BF16)
    return jnp.dot(hits.astype(BF16), earlier, preferred_element_type=F32)


def dispatch_gather(tokens, out_grad, routes, probs, w_one, cap):
    tok_rows, width = tokens.shape
    top = routes.shape[1]
    me = lax.axis_index("expert").astype(F32)
    table = jnp.concatenate([routes.T.astype(BF16), probs.T], axis=0)
    table = jnp.pad(table, ((0, -2 * top % 16), (0, 0)))
    table, rows_x, rows_dy, proj = gather_all(
        lax.axis_size("expert"), cap, top, w_one, table, tokens, out_grad
    )
    table = table.astype(F32)
    mine = table[:, :top] == me
    hits = jnp.any(mine, axis=1)
    prob = jnp.sum(jnp.where(mine, table[:, top : 2 * top], 0.0), axis=1)
    rank = exclusive_rank(hits)
    place = (rank[:, None, :] == jnp.arange(cap, dtype=F32)[None, :, None]) & hits[:, None, :]
    rows_p = jnp.sum(jnp.where(place, prob[:, None, :], 0.0), axis=2).reshape(-1)
    return rows_x, rows_dy, rows_p, proj


def dispatch_exchange(tokens, out_grad, probs, slot, experts, cap):
    tok_rows, width = tokens.shape
    top = slot.shape[1]
    flat = slot.reshape(-1)
    slot_hit = flat[:, None] == jnp.arange(experts * cap, dtype=jnp.int32)[None, :]
    filled = jnp.any(slot_hit, axis=0)
    owner = jnp.sum(jnp.where(slot_hit, jnp.arange(flat.shape[0], dtype=jnp.int32)[:, None], 0), axis=0)
    source = owner // top
    zero = jnp.zeros((), BF16)

    def move(rows):
        return lax.all_to_all(rows, "expert", split_axis=0, concat_axis=0, tiled=True)

    send_x = jnp.where(filled[:, None], tokens[source], zero).reshape(experts, cap, width)
    send_dy = jnp.where(filled[:, None], out_grad[source], zero).reshape(experts, cap, width)
    send_p = jnp.where(filled, probs.reshape(-1)[owner], zero).reshape(experts, cap)
    return (
        move(send_x).reshape(-1, width),
        move(send_dy).reshape(-1, width),
        move(send_p).reshape(-1).astype(F32),
    )


def fused_kernel(top, *refs):
    table_in, x_hbm, dy_hbm, w1_hbm, w2_hbm = refs[:5]
    tok_out, prob_out, g1_out, g2_out = refs[5:9]
    tabs, all_x, all_dy, w1, w2, rows_x, rows_dy, places, chance = refs[9:18]
    slope_up, act_keep, hid_keep, hid_t, pg, xs, xs_t, g1_sum = refs[18:26]
    ret, got, own_t, part_s, part_r = refs[26:31]
    own_sem, w_sem, z_send, z_recv, xs_send, xs_recv, pg_send, pg_recv = refs[31:39]
    fw_send, fw_recv, ret_send, ret_recv, part_send, part_recv, keep_sem = refs[39:]
    ins, outs = (table_in, x_hbm, dy_hbm), (tabs, all_x, all_dy)
    count = 3
    n, tok, width = all_x.shape
    rows = rows_x.shape[1]
    cap = rows // 2
    hidden = w2.shape[0]
    share = width // 4
    half_hidden = hidden // 2
    chips = n // 2
    me, rep = lax.axis_index("expert"), lax.axis_index("dp")
    z, core = me // 2, me % 2
    rep_x = rep + 1 - 2 * (rep % 2)
    rep_y = rep + 2 - 4 * (rep // 2)
    rep_d = 3 - rep
    tile = 256

    loads = [pltpu.make_async_copy(w1_hbm, w1, w_sem.at[0]), pltpu.make_async_copy(w2_hbm, w2, w_sem.at[1])]
    keeps = [pltpu.make_async_copy(ins[a], outs[a].at[me], own_sem.at[a]) for a in range(count)]
    for c in keeps + loads:
        c.start()

    barrier = pltpu.get_barrier_semaphore()
    for i in range(1, n):
        pl.semaphore_signal(
            barrier, inc=1, device_id={"expert": (me + i) % n}, device_id_type=pl.DeviceIdType.MESH
        )
    for target in (rep_x, rep_y, rep_d):
        pl.semaphore_signal(
            barrier, inc=1, device_id={"dp": target}, device_id_type=pl.DeviceIdType.MESH
        )
    pl.semaphore_wait(barrier, n - 1 + 3)

    ways = ((me - core + 1 - core, None), (me + 2, z < chips - 1), (me - 2, z > 0))

    def guarded(ok, body):
        if ok is None:
            body()
        else:
            pl.when(ok)(body)

    def send(src, dst, send_sem, recv_sem, device):
        return pltpu.make_async_remote_copy(
            src_ref=src,
            dst_ref=dst,
            send_sem=send_sem,
            recv_sem=recv_sem,
            device_id=device,
            device_id_type=pl.DeviceIdType.MESH,
        )

    def along(a, slot, hop, way):
        source = ins[a] if hop is None else outs[a].at[slot]
        return send(
            source,
            outs[a].at[slot],
            z_send.at[a, 0 if hop is None else hop, way],
            z_recv.at[a, slot],
            {"expert": ways[way][0]},
        )

    def hops(step):
        return (
            (2 * step - 1, me - 2 * step, z - step >= 0, 1),
            (2 * step, me + 2 * step, z + step < chips, 2),
        )

    def pass_on(a, step):
        for hop, slot, here, way in hops(step):

            def relay(hop=hop, slot=slot, way=way):
                along(a, slot, hop, way).wait_recv()
                pl.when(ways[way][1])(lambda: along(a, slot, hop, way).start())
                along(a, slot, hop, 0).start()

            pl.when(here)(relay)

    def chip_of(k):
        upper = z // 2
        low = z + upper * (3 - 2 * z)
        near = k + low * (1 - k // 2) * (1 - 2 * k)
        return near + upper * (3 - 2 * near)

    def slice_copy(k, i):
        target = (rep_x, rep_y, rep_d)[i]
        return send(
            rows_x.at[k, :, pl.ds(pl.multiple_of(target * share, share), share)],
            xs.at[k * 4 + rep],
            xs_send.at[k, i],
            xs_recv.at[k, rep],
            {"dp": target},
        )

    def slice_wait(k, other):
        send(
            rows_x.at[k, :, pl.ds(0, share)], xs.at[k * 4 + other], xs_send.at[k, 0], xs_recv.at[k, other], {"dp": other}
        ).wait_recv()

    def grad_copy(k, i):
        return send(
            pg.at[k * 4 + rep], pg.at[k * 4 + rep], pg_send.at[k, i], pg_recv.at[k, rep], {"dp": (rep_x, rep_y)[i]}
        )

    def grad_wait(k, other):
        send(pg.at[k * 4 + other], pg.at[k * 4 + other], pg_send.at[k, 0], pg_recv.at[k, other], {"dp": other}).wait_recv()

    def forward_copy(k, i):
        came, goes = ((rep_x, rep_y), (rep_y, rep_x))[i]
        part = pg.at[k * 4 + came, pl.ds(i * cap, cap)]
        return send(part, part, fw_send.at[k, i], fw_recv.at[k, i], {"dp": goes})

    def forward_wait(k):
        for i in range(2):
            part = pg.at[k * 4 + rep_d, pl.ds(i * cap, cap)]
            send(part, part, fw_send.at[k, i], fw_recv.at[k, i], {"dp": (rep_y, rep_x)[i]}).wait_recv()

    def forward(k):
        grad_wait(k, rep_x)
        forward_copy(k, 0).start()
        grad_wait(k, rep_y)
        forward_copy(k, 1).start()

    def return_copy(k, i):
        return send(
            ret.at[k, pl.ds(i * cap, cap)],
            got.at[me],
            ret_send.at[k, i],
            ret_recv.at[me],
            {"expert": 2 * chip_of(k) + i},
        )

    def give_back(k):
        for i in range(2):
            pl.when(2 * chip_of(k) + i != me)(lambda i=i: return_copy(k, i).start())

    def keep_own():
        return pltpu.make_async_copy(ret.at[0, pl.ds(core * cap, cap)], got.at[me], keep_sem)

    for a in range(count):
        for way in (1, 2, 0):
            guarded(ways[way][1], lambda a=a, way=way: along(a, me, None, way).start())

    earlier = lax.broadcasted_iota(jnp.int32, (tok, tok), 0) < lax.broadcasted_iota(jnp.int32, (tok, tok), 1)
    earlier = jnp.where(earlier, 1.0, 0.0).astype(BF16)
    order = lax.broadcasted_iota(jnp.int32, (cap, tok), 0).astype(F32)

    def placing(named, expert):
        hit = jnp.zeros((1, tok), F32)
        prob = jnp.zeros((1, tok), F32)
        for k in range(top):
            match = jnp.where(named[k : k + 1] == expert, 1.0, 0.0)
            hit = hit + match
            prob = prob + match * named[top + k : top + k + 1]
        rank = jnp.dot(
            jnp.broadcast_to(hit, (16, tok)).astype(BF16), earlier, preferred_element_type=F32
        )[0:1]
        return jnp.where(order == rank, 1.0, 0.0) * hit, prob

    nt = (((1,), (1,)), ((), ()))

    def pick(source, target, k, chip):
        def one(j, carry):
            at = pl.ds(pl.multiple_of(j * 512, 512), 512)
            pair = source[pl.ds(2 * chip, 2), :, at].reshape(2 * tok, 512)
            target[k, :, at] = jnp.dot(places[...], pair, preferred_element_type=F32).astype(BF16)
            return carry

        lax.fori_loop(0, width // 512, one, 0)

    def chunk(k, carry):
        chip = chip_of(k)
        other = 2 * chip + 1 - core

        def relays(a):
            pl.when(k > 0)(lambda: pass_on(a, k))
            pl.when(k == 0)(keeps[a].wait)
            along(a, other, 0, 0).wait_recv()

        relays(0)
        relays(1)
        blocks, probs = [], []
        blank = jnp.zeros((cap, tok), F32)
        for i in range(2):
            place, prob = placing(tabs[2 * chip + i].astype(F32), me.astype(F32))
            blocks.append(jnp.concatenate([blank] * i + [place] + [blank] * (1 - i), axis=1))
            probs.append(jnp.sum(place * prob, axis=1, keepdims=True))
        places[...] = jnp.concatenate(blocks, axis=0).astype(BF16)
        chance[...] = jnp.broadcast_to(jnp.concatenate(probs, axis=0), chance.shape)
        pick(all_x, rows_x, k, chip)
        for i in range(3):
            slice_copy(k, i).start()
        xs[k * 4 + rep] = rows_x[k, :, pl.ds(pl.multiple_of(rep * share, share), share)]
        pl.when(k == 0)(loads[0].wait)

        def units(j, carry):
            at = pl.ds(pl.multiple_of(j * tile, tile), tile)
            up_at = pl.ds(pl.multiple_of(hidden + j * tile, tile), tile)
            gate = jnp.dot(rows_x[k], w1[:, at], preferred_element_type=F32)
            upper = jnp.dot(rows_x[k], w1[:, up_at], preferred_element_type=F32)
            sig = jax.nn.sigmoid(gate)
            act = gate * sig
            hid = (act * upper).astype(BF16)
            scaled = chance[:, 0:1] * hid.astype(F32)
            slope_up[:, at] = upper * (sig * (1.0 + gate * (1.0 - sig)))
            act_keep[:, at] = act
            hid_keep[:, at] = hid
            hid_t[at, pl.ds(pl.multiple_of(k * rows, rows), rows)] = scaled.T.astype(BF16)
            return carry

        lax.fori_loop(0, hidden // tile, units, 0)
        pl.when(k > 0)(lambda: forward(k - 1))
        relays(2)
        pick(all_dy, rows_dy, k, chip)
        pl.when(k == 0)(loads[1].wait)

        def backs(j, total):
            at = pl.ds(pl.multiple_of(j * tile, tile), tile)
            up_at = pl.ds(pl.multiple_of(hidden + j * tile, tile), tile)
            back = lax.dot_general(rows_dy[k], w2[at, :], nt, preferred_element_type=F32)
            hid_grad = chance[:, 0:1] * back
            pg[k * 4 + rep, :, at] = (hid_grad * slope_up[:, at]).astype(BF16)
            pg[k * 4 + rep, :, up_at] = (hid_grad * act_keep[:, at]).astype(BF16)
            return total + jnp.sum(back * hid_keep[:, at].astype(F32), axis=1, keepdims=True)

        dprob = lax.fori_loop(0, hidden // tile, backs, jnp.zeros((rows, 1), F32))
        ret[k, :, pl.ds(width, 128)] = jnp.broadcast_to(dprob, (rows, 128)).astype(BF16)
        for i in range(2):
            grad_copy(k, i).start()

        def rows_back(j, carry):
            at = pl.ds(pl.multiple_of(j * tile, tile), tile)
            ret[k, :, at] = lax.dot_general(
                pg[k * 4 + rep], w1[at, :], nt, preferred_element_type=F32
            ).astype(BF16)
            return carry

        lax.fori_loop(0, width // tile, rows_back, 0)

        @pl.when(k == 0)
        def _():
            give_back(0)
            keep_own().start()

        @pl.when(k == 2)
        def _():
            give_back(1)
            give_back(2)

        pl.when(k == 3)(lambda: give_back(3))
        return carry

    lax.fori_loop(0, chips, chunk, 0)

    def piece(column, half):
        dy = rows_dy[:, :, pl.ds(pl.multiple_of(column * share, share), share)].reshape(chips * rows, share)
        return jnp.dot(
            hid_t[half * half_hidden : (half + 1) * half_hidden], dy, preferred_element_type=F32
        )

    def part_copy(i, target):
        return send(part_s.at[i], part_r.at[i], part_send.at[i], part_recv.at[i], {"dp": target})

    sides = (rep_x, rep_y, rep_x, rep_y, rep_y, rep_x)
    for i, column in enumerate((rep_d, rep_d, rep_x, rep_y)):
        part_s[i] = piece(column, i % 2).astype(BF16)
        part_copy(i, sides[i]).start()

    def turn(k):
        for r in range(4):
            pl.when(r != rep)(lambda r=r: slice_wait(k, r))
            xs_t[:, (k * 4 + r) * rows : (k * 4 + r + 1) * rows] = xs[k * 4 + r].astype(F32).T.astype(BF16)

    early = 4 * (chips - 1)
    for k in range(chips - 1):
        turn(k)
        forward_wait(k)

    def sums(j, carry):
        at = pl.ds(pl.multiple_of(j * tile, tile), tile)
        g1_sum[:, at] = jnp.dot(
            xs_t[:, : early * rows], pg[0:early, :, at].reshape(early * rows, tile), preferred_element_type=F32
        )
        return carry

    lax.fori_loop(0, 2 * hidden // tile, sums, 0)
    forward(chips - 1)
    for half in range(2):
        part_copy(half, sides[half]).wait_recv()
        mine = piece((rep_y, rep_x)[half], half)
        part_s[4 + half] = (mine + part_r[half].astype(F32)).astype(BF16)
        part_copy(4 + half, sides[4 + half]).start()

    named = tabs[me].astype(F32)
    owns = [placing(named, float(e))[0] for e in range(n)]
    for c in range(chips):
        own_t[:, c * 2 * cap : (c + 1) * 2 * cap] = (
            jnp.concatenate([owns[2 * c], owns[2 * c + 1]], axis=0).T.astype(BF16)
        )
    turn(chips - 1)
    keep_own().wait()
    for e in range(n):
        pl.when(e != me)(
            lambda e=e: send(
                ret.at[0, pl.ds(0, cap)], got.at[e], ret_send.at[0, 0], ret_recv.at[e], {"expert": e}
            ).wait_recv()
        )

    def combine(j, carry):
        at = pl.ds(pl.multiple_of(j * tile, tile), tile)
        tok_out[:, at] = jnp.dot(
            own_t[...], got[:, :, at].reshape(n * cap, tile), preferred_element_type=F32
        ).astype(BF16)
        return carry

    lax.fori_loop(0, width // tile, combine, 0)
    found = [jnp.zeros((1, tok), F32)] * top
    for e in range(n):
        value = jnp.sum(owns[e] * got[e, :, width : width + 128].astype(F32), axis=0, keepdims=True)
        found = [found[k] + jnp.where(named[k : k + 1] == float(e), value, 0.0) for k in range(top)]
    prob_out[...] = jnp.concatenate(found + [jnp.zeros((8 - top, tok), F32)], axis=0)

    grad_wait_last = chips - 1
    forward_wait(grad_wait_last)

    def finals(j, carry):
        at = pl.ds(pl.multiple_of(j * tile, tile), tile)
        g1_out[:, at] = (
            g1_sum[:, at]
            + jnp.dot(
                xs_t[:, early * rows :], pg[early : early + 4, :, at].reshape(4 * rows, tile), preferred_element_type=F32
            )
        ).astype(BF16)
        return carry

    lax.fori_loop(0, 2 * hidden // tile, finals, 0)
    for half in range(2):
        mine = piece(rep, half)
        part_copy(2 + half, sides[2 + half]).wait_recv()
        part_copy(4 + half, sides[4 + half]).wait_recv()
        g2_out[half * half_hidden : (half + 1) * half_hidden, :] = (
            mine + part_r[2 + half].astype(F32) + part_r[4 + half].astype(F32)
        ).astype(BF16)

    for a in range(count):
        for way in range(3):
            guarded(ways[way][1], lambda a=a, way=way: along(a, me, None, way).wait_send())

    def drain(step, carry):
        for a in range(count):
            for hop, slot, here, way in hops(step):

                def one(a=a, hop=hop, slot=slot, way=way):
                    pl.when(ways[way][1])(lambda: along(a, slot, hop, way).wait_send())
                    along(a, slot, hop, 0).wait_send()

                pl.when(here)(one)
        return carry

    lax.fori_loop(1, chips, drain, 0)

    def drain_chunk(k, carry):
        for i in range(3):
            slice_copy(k, i).wait_send()
        for i in range(2):
            grad_copy(k, i).wait_send()
            forward_copy(k, i).wait_send()
            pl.when(2 * chip_of(k) + i != me)(lambda i=i: return_copy(k, i).wait_send())
        return carry

    lax.fori_loop(0, chips, drain_chunk, 0)
    for i in range(6):
        part_copy(i, sides[i]).wait_send()


def fused(tokens, out_grad, routes, probs, w_one, w_two, n, cap):
    tok, width = tokens.shape
    top, hidden = routes.shape[1], w_two.shape[0]
    table = jnp.concatenate([routes.T.astype(BF16), probs.T], axis=0)
    table = jnp.pad(table, ((0, -2 * top % 16), (0, 0)))
    chips, rows, share = n // 2, 2 * cap, width // 4
    vmem, hbm = pl.BlockSpec(memory_space=pltpu.VMEM), pl.BlockSpec(memory_space=pl.ANY)
    dma = pltpu.SemaphoreType.DMA
    token_grad, prob, share_one, share_two = pl.pallas_call(
        lambda *refs: fused_kernel(top, *refs),
        out_shape=[
            jax.ShapeDtypeStruct((tok, width), BF16),
            jax.ShapeDtypeStruct((8, tok), F32),
            jax.ShapeDtypeStruct((share, 2 * hidden), BF16),
            jax.ShapeDtypeStruct((hidden, share), BF16),
        ],
        in_specs=[vmem] + [hbm] * 4,
        out_specs=[vmem] * 4,
        scratch_shapes=[
            pltpu.VMEM((n,) + table.shape, BF16),
            pltpu.VMEM((n, tok, width), BF16),
            pltpu.VMEM((n, tok, width), BF16),
            pltpu.VMEM((width, 2 * hidden), BF16),
            pltpu.VMEM((hidden, width), BF16),
            pltpu.VMEM((chips, rows, width), BF16),
            pltpu.VMEM((chips, rows, width), BF16),
            pltpu.VMEM((rows, 2 * tok), BF16),
            pltpu.VMEM((rows, 128), F32),
            pltpu.VMEM((rows, hidden), F32),
            pltpu.VMEM((rows, hidden), F32),
            pltpu.VMEM((rows, hidden), BF16),
            pltpu.VMEM((hidden, chips * rows), BF16),
            pltpu.VMEM((chips * 4, rows, 2 * hidden), BF16),
            pltpu.VMEM((chips * 4, rows, share), BF16),
            pltpu.VMEM((share, chips * 4 * rows), BF16),
            pltpu.VMEM((share, 2 * hidden), F32),
            pltpu.VMEM((chips, rows, width + 128), BF16),
            pltpu.VMEM((n, cap, width + 128), BF16),
            pltpu.VMEM((tok, n * cap), BF16),
            pltpu.VMEM((6, hidden // 2, share), BF16),
            pltpu.VMEM((6, hidden // 2, share), BF16),
            dma((3,)),
            dma((2,)),
            dma((3, n - 1, 3)),
            dma((3, n)),
            dma((chips, 3)),
            dma((chips, 4)),
            dma((chips, 2)),
            dma((chips, 4)),
            dma((chips, 2)),
            dma((chips, 2)),
            dma((chips, 2)),
            dma((n,)),
            dma((6,)),
            dma((6,)),
            dma,
        ],
        compiler_params=pltpu.CompilerParams(
            collective_id=0, has_side_effects=True, vmem_limit_bytes=62 * 1024 * 1024
        ),
    )(table, tokens, out_grad, w_one, w_two)
    return token_grad, prob[:top].T.astype(BF16), share_one[None], share_two[None]


def swap(value, flip):
    return lax.ppermute(value, "dp", [(i, i ^ flip) for i in range(4)])


def square_first(piece):
    got = []
    for rest in (True, False):
        for half, side in ((0, 1), (1, 2)):
            flip = 3 if rest else side
            got.append(swap(piece(flip, half).astype(BF16), side))
    return got


def square_second(piece, got):
    sent = []
    for half, side in ((0, 2), (1, 1)):
        total = (piece(side, half) + got[half].astype(F32)).astype(BF16)
        sent.append(swap(total, side))
    return [
        (piece(0, half) + got[2 + half].astype(F32) + sent[half].astype(F32)).astype(BF16)
        for half in range(2)
    ]


def shards(tokens, out_grad, routes, probs, w_in, w_out):
    tok_rows, width = tokens.shape
    top = routes.shape[1]
    n_groups = lax.axis_size("expert")
    experts = n_groups * w_in.shape[0]
    hidden = w_out.shape[1]
    cap = 4 * tok_rows * top // (3 * experts)
    w_one, w_two = w_in[0], w_out[0]
    if n_groups == 8 and lax.axis_size("dp") == 4:
        return fused(tokens, out_grad, routes, probs, w_one, w_two, n_groups, cap)

    names = jnp.arange(experts, dtype=jnp.int32)
    named = routes[:, :, None] == names[None, None, :]
    hits = jnp.any(named, axis=1)
    later = (jnp.arange(tok_rows)[:, None] > jnp.arange(tok_rows)[None, :]).astype(BF16)
    rank = jnp.dot(later, hits.astype(BF16), preferred_element_type=F32)
    own_rank = jnp.sum(jnp.where(named, rank[:, None, :], 0.0), axis=2).astype(jnp.int32)
    slot = routes * cap + own_rank

    if experts <= 16:
        rows_x, rows_dy, rows_p, proj = dispatch_gather(tokens, out_grad, routes, probs, w_one, cap)
    else:
        rows_x, rows_dy, rows_p = dispatch_exchange(tokens, out_grad, probs, slot, experts, cap)
        proj = jnp.dot(rows_x, w_one, preferred_element_type=F32)
    rows_p = rows_p[:, None]
    gate, upper = proj[:, :hidden], proj[:, hidden:]
    sig = jax.nn.sigmoid(gate)
    act = gate * sig
    hid = (act * upper).astype(BF16)
    scaled = (rows_p * hid.astype(F32)).astype(BF16)
    replicas = lax.axis_size("dp")
    part = width // replicas
    at = lax.axis_index("dp")
    contract = (((0,), (0,)), ((), ()))

    def piece_two(flip, half):
        cut = lax.dynamic_slice_in_dim(rows_dy, (at ^ flip) * part, part, axis=1)
        units = scaled[:, half * (hidden // 2) : (half + 1) * (hidden // 2)]
        return lax.dot_general(units, cut, contract, preferred_element_type=F32)

    if replicas == 4:
        first_two = square_first(piece_two)
    else:
        grad_two = lax.dot_general(scaled, rows_dy, contract, preferred_element_type=F32).astype(BF16)
        share_two = lax.psum_scatter(grad_two, "dp", scatter_dimension=1, tiled=True)

    back = lax.dot_general(rows_dy, w_two, (((1,), (1,)), ((), ())), preferred_element_type=F32)
    dprob = jnp.sum(back * hid.astype(F32), axis=1).astype(BF16)
    hid_grad = rows_p * back
    proj_grad = jnp.concatenate(
        [hid_grad * upper * (sig * (1.0 + gate * (1.0 - sig))), hid_grad * act], axis=1
    ).astype(BF16)

    def piece_one(flip, half):
        cut = lax.dynamic_slice_in_dim(rows_x, (at ^ flip) * part, part, axis=1)
        units = proj_grad[:, half * hidden : (half + 1) * hidden]
        return lax.dot_general(cut, units, contract, preferred_element_type=F32)

    if replicas == 4:
        first_one = square_first(piece_one)
        second_two = square_second(piece_two, first_two)
        second_one = square_second(piece_one, first_one)
        share_two = jnp.concatenate(second_two, axis=0)
        share_one = jnp.concatenate(second_one, axis=1)
    else:
        grad_one = lax.dot_general(rows_x, proj_grad, contract, preferred_element_type=F32).astype(BF16)
        share_one = lax.psum_scatter(grad_one, "dp", scatter_dimension=0, tiled=True)

    row_grad = lax.dot_general(
        proj_grad, w_one, (((1,), (1,)), ((), ())), preferred_element_type=F32
    ).astype(BF16)
    back_x = lax.all_to_all(
        row_grad.reshape(n_groups, cap, width), "expert", split_axis=0, concat_axis=0, tiled=True
    ).reshape(experts * cap, width)
    back_p = lax.all_to_all(
        dprob.reshape(n_groups, cap), "expert", split_axis=0, concat_axis=0, tiled=True
    ).reshape(-1)
    slots = jnp.arange(experts * cap, dtype=jnp.int32)
    held = slot[:, :, None] == slots[None, None, :]
    prob_grad = jnp.sum(jnp.where(held, back_p.astype(F32), 0.0), axis=2).astype(BF16)
    token_grad = jnp.dot(
        jnp.any(held, axis=1).astype(BF16), back_x, preferred_element_type=F32
    ).astype(BF16)
    return token_grad, prob_grad, share_one[None], share_two[None]


def solution(mesh):
    return jax.shard_map(
        shards,
        mesh=mesh,
        in_specs=(
            P(("dp", "expert"), None),
            P(("dp", "expert"), None),
            P(("dp", "expert"), None),
            P(("dp", "expert"), None),
            P("expert", None, None),
            P("expert", None, None),
        ),
        out_specs=(
            P(("dp", "expert"), None),
            P(("dp", "expert"), None),
            P("expert", "dp", None),
            P("expert", None, "dp"),
        ),
        check_vma=False,
    )
```

```python
import jax
import jax.numpy as jnp
from jax import lax
from jax.experimental import pallas as pl
from jax.experimental.pallas import tpu as pltpu
from jax.sharding import PartitionSpec as P

F32 = jnp.float32
BF16 = jnp.bfloat16


def gather_kernel(n, cap, top, *refs):
    count = 3
    ins, w_hbm = refs[:count], refs[count]
    table_out, rows_x, rows_dy, proj = refs[count + 1 : count + 5]
    all_x, all_dy, w_vmem, w_sem, own_sem, send_sem, recv_sem = refs[count + 5 :]
    outs = (table_out, all_x, all_dy)
    load_w = pltpu.make_async_copy(w_hbm, w_vmem, w_sem)
    load_w.start()
    chips = n // 2
    me = lax.axis_index("expert")
    z, core = me // 2, me % 2
    ways = (
        (me - core + 1 - core, None),
        (me + 2, z < chips - 1),
        (me - 2, z > 0),
    )

    def guarded(ok, body):
        if ok is None:
            body()
        else:
            pl.when(ok)(body)

    barrier = pltpu.get_barrier_semaphore()
    for target, ok in ways:
        guarded(ok, lambda target=target: pl.semaphore_signal(
            barrier, inc=1, device_id={"expert": target}, device_id_type=pl.DeviceIdType.MESH
        ))
    peers = 1 + (z < chips - 1).astype(jnp.int32) + (z > 0).astype(jnp.int32)
    pl.semaphore_wait(barrier, peers)

    def copy(a, slot, hop, way):
        source = ins[a] if hop is None else outs[a].at[slot]
        return pltpu.make_async_remote_copy(
            src_ref=source,
            dst_ref=outs[a].at[slot],
            send_sem=send_sem.at[a, 0 if hop is None else hop, way],
            recv_sem=recv_sem.at[a, slot],
            device_id={"expert": ways[way][0]},
            device_id_type=pl.DeviceIdType.MESH,
        )

    def locals_():
        return [pltpu.make_async_copy(ins[a], outs[a].at[me], own_sem.at[a]) for a in range(count)]

    for c in locals_():
        c.start()
    hops = []
    for step in range(1, chips):
        hops.append((2 * step - 1, me - 2 * step, z - step >= 0, 1))
        hops.append((2 * step, me + 2 * step, z + step < chips, 2))
    def pick(rows_in, rows_out):
        tok = rows_in.shape[1]
        earlier = (
            lax.broadcasted_iota(jnp.int32, (tok, tok), 0) < lax.broadcasted_iota(jnp.int32, (tok, tok), 1)
        )
        earlier = jnp.where(earlier, 1.0, 0.0).astype(BF16)
        order = lax.broadcasted_iota(jnp.int32, (cap, tok), 0).astype(F32)

        def one(b, carry):
            named = table_out[b].astype(F32)
            hit = jnp.zeros((1, tok), F32)
            for k in range(top):
                hit = hit + jnp.where(named[k : k + 1] == me.astype(F32), 1.0, 0.0)
            rank = jnp.dot(
                jnp.broadcast_to(hit, (16, tok)).astype(BF16), earlier, preferred_element_type=F32
            )[0:1]
            place = jnp.where(order == rank, 1.0, 0.0) * hit
            rows_out[pl.ds(pl.multiple_of(b * cap, cap), cap), :] = jnp.dot(
                place.astype(BF16), rows_in[b], preferred_element_type=F32
            ).astype(BF16)
            return carry

        lax.fori_loop(0, n, one, 0)

    def send_own(a):
        for way in (1, 2, 0):
            guarded(ways[way][1], lambda a=a, way=way: copy(a, me, None, way).start())

    def pass_on(a):
        for hop, slot, here, way in hops:

            def relay(a=a, hop=hop, slot=slot, way=way):
                copy(a, slot, hop, way).wait_recv()
                pl.when(ways[way][1])(lambda: copy(a, slot, hop, way).start())
                copy(a, slot, hop, 0).start()

            pl.when(here)(relay)

    def finish(a):
        for chip in range(chips):
            copy(a, 2 * chip + 1 - core, 0, 0).wait_recv()

    send_own(0)
    send_own(1)
    pass_on(0)
    pass_on(1)
    send_own(2)
    for c in locals_():
        c.wait()
    finish(0)
    finish(1)
    load_w.wait()
    tile = 256
    steps = proj.shape[1] // tile
    width = steps // len(hops) if steps >= len(hops) else 0

    def columns(first, last):
        def one(i, carry):
            at = pl.ds(pl.multiple_of(i * tile, tile), tile)
            proj[:, at] = jnp.dot(rows_x[...], w_vmem[:, at], preferred_element_type=F32)
            return carry

        lax.fori_loop(first, last, one, 0)

    pick(all_x, rows_x)
    for i, (hop, slot, here, way) in enumerate(hops):

        def relay(hop=hop, slot=slot, way=way):
            copy(2, slot, hop, way).wait_recv()
            pl.when(ways[way][1])(lambda: copy(2, slot, hop, way).start())
            copy(2, slot, hop, 0).start()

        pl.when(here)(relay)
        columns(i * width, (i + 1) * width if i < len(hops) - 1 else steps)
    finish(2)
    pick(all_dy, rows_dy)
    for a in range(count):
        for way in range(3):
            guarded(ways[way][1], lambda a=a, way=way: copy(a, me, None, way).wait_send())
        for hop, slot, here, way in hops:

            def drain(a=a, hop=hop, slot=slot, way=way):
                pl.when(ways[way][1])(lambda: copy(a, slot, hop, way).wait_send())
                copy(a, slot, hop, 0).wait_send()

            pl.when(here)(drain)


def gather_all(n, cap, top, w_one, *arrays):
    table, rows = arrays[:2]
    vmem, width = pl.BlockSpec(memory_space=pltpu.VMEM), rows.shape[1]
    return pl.pallas_call(
        lambda *refs: gather_kernel(n, cap, top, *refs),
        out_shape=[
            jax.ShapeDtypeStruct((n,) + table.shape, BF16),
            jax.ShapeDtypeStruct((n * cap, width), BF16),
            jax.ShapeDtypeStruct((n * cap, width), BF16),
            jax.ShapeDtypeStruct((n * cap, w_one.shape[1]), F32),
        ],
        in_specs=[vmem] * 3 + [pl.BlockSpec(memory_space=pl.ANY)],
        out_specs=[vmem] * 4,
        scratch_shapes=[
            pltpu.VMEM((n,) + rows.shape, BF16),
            pltpu.VMEM((n,) + rows.shape, BF16),
            pltpu.VMEM(w_one.shape, BF16),
            pltpu.SemaphoreType.DMA,
            pltpu.SemaphoreType.DMA((3,)),
            pltpu.SemaphoreType.DMA((3, n - 1, 3)),
            pltpu.SemaphoreType.DMA((3, n)),
        ],
        compiler_params=pltpu.CompilerParams(
            collective_id=0, has_side_effects=True, vmem_limit_bytes=48 * 1024 * 1024
        ),
    )(*arrays, w_one)


def exclusive_rank(hits):
    rows = hits.shape[1]
    earlier = (jnp.arange(rows)[:, None] < jnp.arange(rows)[None, :]).astype(BF16)
    return jnp.dot(hits.astype(BF16), earlier, preferred_element_type=F32)


def dispatch_gather(tokens, out_grad, routes, probs, w_one, cap):
    tok_rows, width = tokens.shape
    top = routes.shape[1]
    me = lax.axis_index("expert").astype(F32)
    table = jnp.concatenate([routes.T.astype(BF16), probs.T], axis=0)
    table = jnp.pad(table, ((0, -2 * top % 16), (0, 0)))
    table, rows_x, rows_dy, proj = gather_all(
        lax.axis_size("expert"), cap, top, w_one, table, tokens, out_grad
    )
    table = table.astype(F32)
    mine = table[:, :top] == me
    hits = jnp.any(mine, axis=1)
    prob = jnp.sum(jnp.where(mine, table[:, top : 2 * top], 0.0), axis=1)
    rank = exclusive_rank(hits)
    place = (rank[:, None, :] == jnp.arange(cap, dtype=F32)[None, :, None]) & hits[:, None, :]
    rows_p = jnp.sum(jnp.where(place, prob[:, None, :], 0.0), axis=2).reshape(-1)
    return rows_x, rows_dy, rows_p, proj


def dispatch_exchange(tokens, out_grad, probs, slot, experts, cap):
    tok_rows, width = tokens.shape
    top = slot.shape[1]
    flat = slot.reshape(-1)
    slot_hit = flat[:, None] == jnp.arange(experts * cap, dtype=jnp.int32)[None, :]
    filled = jnp.any(slot_hit, axis=0)
    owner = jnp.sum(jnp.where(slot_hit, jnp.arange(flat.shape[0], dtype=jnp.int32)[:, None], 0), axis=0)
    source = owner // top
    zero = jnp.zeros((), BF16)

    def move(rows):
        return lax.all_to_all(rows, "expert", split_axis=0, concat_axis=0, tiled=True)

    send_x = jnp.where(filled[:, None], tokens[source], zero).reshape(experts, cap, width)
    send_dy = jnp.where(filled[:, None], out_grad[source], zero).reshape(experts, cap, width)
    send_p = jnp.where(filled, probs.reshape(-1)[owner], zero).reshape(experts, cap)
    return (
        move(send_x).reshape(-1, width),
        move(send_dy).reshape(-1, width),
        move(send_p).reshape(-1).astype(F32),
    )


def fused_kernel(top, *refs):
    routes_in, probs_in, x_hbm, dy_hbm, w1_hbm, w2_hbm = refs[:6]
    tok_out, prob_out, g1_out, g2_out = refs[6:10]
    tabs, all_x, all_dy, w1, w2, rows_x, rows_dy, places, chance = refs[10:19]
    slope_up, act_keep, hid_keep, hid_t, pg, xs, xs_t, g1_sum = refs[19:27]
    ret, ret_p, got, got_p, own_t, part_s, part_r = refs[27:34]
    own_sem, w_sem, z_send, z_recv, xs_send, xs_recv, pg_send, pg_recv = refs[34:42]
    fw_send, fw_recv, ret_send, ret_recv, part_send, part_recv, keep_sem = refs[42:]
    count = 6
    n, tok, width = all_x.shape
    rows = rows_x.shape[1]
    cap = rows // 2
    hidden = w2.shape[0]
    share = width // 4
    half_hidden = hidden // 2
    chips = n // 2
    me, rep = lax.axis_index("expert"), lax.axis_index("dp")
    z, core = me // 2, me % 2
    rep_x = rep + 1 - 2 * (rep % 2)
    rep_y = rep + 2 - 4 * (rep // 2)
    rep_d = 3 - rep
    tile = 256

    columns = (rep_d, rep_x, rep_y, rep)

    def quarter(i):
        return pl.ds(pl.multiple_of(columns[i] * share, share), share)

    def own(a):
        return (tabs.at[me], x_hbm)[a] if a < 2 else dy_hbm.at[:, quarter(a - 2)]

    def held(a, slot):
        return (tabs, all_x)[a].at[slot] if a < 2 else all_dy.at[slot, :, quarter(a - 2)]

    loads = [pltpu.make_async_copy(w1_hbm, w1, w_sem.at[0]), pltpu.make_async_copy(w2_hbm, w2, w_sem.at[1])]
    keeps = [
        pltpu.make_async_copy(x_hbm, all_x.at[me], own_sem.at[0]),
        pltpu.make_async_copy(dy_hbm, all_dy.at[me], own_sem.at[1]),
    ]
    for c in keeps + loads:
        c.start()
    tabs[me] = jnp.concatenate(
        [routes_in[...].astype(F32), probs_in[...].astype(F32), jnp.zeros((16 - 2 * top, tok), F32)], axis=0
    ).astype(BF16)

    barrier = pltpu.get_barrier_semaphore()
    for i in range(1, n):
        pl.semaphore_signal(
            barrier, inc=1, device_id={"expert": (me + i) % n}, device_id_type=pl.DeviceIdType.MESH
        )
    for target in (rep_x, rep_y, rep_d):
        pl.semaphore_signal(
            barrier, inc=1, device_id={"dp": target}, device_id_type=pl.DeviceIdType.MESH
        )
    pl.semaphore_wait(barrier, n - 1 + 3)

    ways = ((me - core + 1 - core, None), (me + 2, z < chips - 1), (me - 2, z > 0))

    def guarded(ok, body):
        if ok is None:
            body()
        else:
            pl.when(ok)(body)

    def send(src, dst, send_sem, recv_sem, device):
        return pltpu.make_async_remote_copy(
            src_ref=src,
            dst_ref=dst,
            send_sem=send_sem,
            recv_sem=recv_sem,
            device_id=device,
            device_id_type=pl.DeviceIdType.MESH,
        )

    def along(a, slot, hop, way):
        source = own(a) if hop is None else held(a, slot)
        return send(
            source,
            held(a, slot),
            z_send.at[a, 0 if hop is None else hop, way],
            z_recv.at[a, slot],
            {"expert": ways[way][0]},
        )

    def hops(step):
        return (
            (2 * step - 1, me - 2 * step, z - step >= 0, 1),
            (2 * step, me + 2 * step, z + step < chips, 2),
        )

    def pass_on(a, step):
        for hop, slot, here, way in hops(step):

            def relay(hop=hop, slot=slot, way=way):
                along(a, slot, hop, way).wait_recv()
                pl.when(ways[way][1])(lambda: along(a, slot, hop, way).start())
                along(a, slot, hop, 0).start()

            pl.when(here)(relay)

    def chip_of(k):
        upper = z // 2
        low = z + upper * (3 - 2 * z)
        near = k + low * (1 - k // 2) * (1 - 2 * k)
        return near + upper * (3 - 2 * near)

    def slice_copy(k, i):
        target = (rep_x, rep_y, rep_d)[i]
        return send(
            rows_x.at[k, :, pl.ds(pl.multiple_of(target * share, share), share)],
            xs.at[k * 4 + rep],
            xs_send.at[k, i],
            xs_recv.at[k, rep],
            {"dp": target},
        )

    def slice_wait(k, other):
        send(
            rows_x.at[k, :, pl.ds(0, share)], xs.at[k * 4 + other], xs_send.at[k, 0], xs_recv.at[k, other], {"dp": other}
        ).wait_recv()

    def grad_copy(k, i):
        return send(
            pg.at[k * 4 + rep], pg.at[k * 4 + rep], pg_send.at[k, i], pg_recv.at[k, rep], {"dp": (rep_x, rep_y)[i]}
        )

    def grad_wait(k, other):
        send(pg.at[k * 4 + other], pg.at[k * 4 + other], pg_send.at[k, 0], pg_recv.at[k, other], {"dp": other}).wait_recv()

    def forward_copy(k, i):
        came, goes = ((rep_x, rep_y), (rep_y, rep_x))[i]
        part = pg.at[k * 4 + came, pl.ds(i * cap, cap)]
        return send(part, part, fw_send.at[k, i], fw_recv.at[k, i], {"dp": goes})

    def forward_wait(k):
        for i in range(2):
            part = pg.at[k * 4 + rep_d, pl.ds(i * cap, cap)]
            send(part, part, fw_send.at[k, i], fw_recv.at[k, i], {"dp": (rep_y, rep_x)[i]}).wait_recv()

    def forward(k):
        grad_wait(k, rep_x)
        forward_copy(k, 0).start()
        grad_wait(k, rep_y)
        forward_copy(k, 1).start()

    def return_copy(k, i):
        return send(
            ret.at[k, pl.ds(i * cap, cap)],
            got.at[me],
            ret_send.at[k, i],
            ret_recv.at[me],
            {"expert": 2 * chip_of(k) + i},
        )

    def return_prob(k, i):
        return send(
            ret_p.at[k], got_p.at[me], ret_send.at[k, 2 + i], ret_recv.at[n + me], {"expert": 2 * chip_of(k) + i}
        )

    def give_back(k):
        for i in range(2):

            @pl.when(2 * chip_of(k) + i != me)
            def _(i=i):
                return_prob(k, i).start()
                return_copy(k, i).start()

    def keep_own():
        return [
            pltpu.make_async_copy(ret.at[0, pl.ds(core * cap, cap)], got.at[me], keep_sem.at[0]),
            pltpu.make_async_copy(ret_p.at[0], got_p.at[me], keep_sem.at[1]),
        ]

    def piece(column, half):
        dy = rows_dy[:, :, pl.ds(pl.multiple_of(column * share, share), share)].reshape(chips * rows, share)
        return jnp.dot(
            hid_t[half * half_hidden : (half + 1) * half_hidden], dy, preferred_element_type=F32
        )

    sides = (rep_x, rep_y, rep_x, rep_y, rep_y, rep_x)

    def part_copy(i):
        return send(part_s.at[i], part_r.at[i], part_send.at[i], part_recv.at[i], {"dp": sides[i]})

    def first_parts(i):
        for slot in ((0, 1), (2,), (3,), ())[i]:
            part_s[slot] = piece(columns[i], slot % 2).astype(BF16)
            part_copy(slot).start()

    for a in range(count):
        for way in (1, 2, 0):
            guarded(ways[way][1], lambda a=a, way=way: along(a, me, None, way).start())

    earlier = lax.broadcasted_iota(jnp.int32, (tok, tok), 0) < lax.broadcasted_iota(jnp.int32, (tok, tok), 1)
    earlier = jnp.where(earlier, 1.0, 0.0).astype(BF16)
    order = lax.broadcasted_iota(jnp.int32, (cap, tok), 0).astype(F32)

    def placing(named, expert):
        hit = jnp.zeros((1, tok), F32)
        prob = jnp.zeros((1, tok), F32)
        for k in range(top):
            match = jnp.where(named[k : k + 1] == expert, 1.0, 0.0)
            hit = hit + match
            prob = prob + match * named[top + k : top + k + 1]
        rank = jnp.dot(
            jnp.broadcast_to(hit, (16, tok)).astype(BF16), earlier, preferred_element_type=F32
        )[0:1]
        return jnp.where(order == rank, 1.0, 0.0) * hit, prob

    nt = (((1,), (1,)), ((), ()))

    def pick(source, target, k, chip, column):
        at = pl.ds(pl.multiple_of(column * share, share), share)
        pair = source[pl.ds(2 * chip, 2), :, at].reshape(2 * tok, share)
        target[k, :, at] = jnp.dot(places[...], pair, preferred_element_type=F32).astype(BF16)

    def chunk(k, carry):
        chip = chip_of(k)
        other = 2 * chip + 1 - core

        def relays(a):
            pl.when(k > 0)(lambda: pass_on(a, k))
            if a in (1, 2):
                pl.when(k == 0)(keeps[a - 1].wait)
            along(a, other, 0, 0).wait_recv()

        relays(0)
        relays(1)
        blocks, probs = [], []
        blank = jnp.zeros((cap, tok), F32)
        for i in range(2):
            place, prob = placing(tabs[2 * chip + i].astype(F32), me.astype(F32))
            blocks.append(jnp.concatenate([blank] * i + [place] + [blank] * (1 - i), axis=1))
            probs.append(jnp.sum(place * prob, axis=1, keepdims=True))
        places[...] = jnp.concatenate(blocks, axis=0).astype(BF16)
        chance[...] = jnp.broadcast_to(jnp.concatenate(probs, axis=0), chance.shape)
        for i in range(4):
            pick(all_x, rows_x, k, chip, i)
        for i in range(3):
            slice_copy(k, i).start()
        xs[k * 4 + rep] = rows_x[k, :, pl.ds(pl.multiple_of(rep * share, share), share)]
        pl.when(k == 0)(loads[0].wait)

        def units(j, carry):
            at = pl.ds(pl.multiple_of(j * tile, tile), tile)
            up_at = pl.ds(pl.multiple_of(hidden + j * tile, tile), tile)
            gate = jnp.dot(rows_x[k], w1[:, at], preferred_element_type=F32)
            upper = jnp.dot(rows_x[k], w1[:, up_at], preferred_element_type=F32)
            sig = jax.nn.sigmoid(gate)
            act = gate * sig
            hid = (act * upper).astype(BF16)
            scaled = chance[:, 0:1] * hid.astype(F32)
            slope_up[:, at] = upper * (sig * (1.0 + gate * (1.0 - sig)))
            act_keep[:, at] = act
            hid_keep[:, at] = hid
            hid_t[at, pl.ds(pl.multiple_of(k * rows, rows), rows)] = scaled.T.astype(BF16)
            return carry

        lax.fori_loop(0, hidden // tile, units, 0)
        pl.when(k > 0)(lambda: forward(k - 1))
        for i in range(4):
            relays(2 + i)
            pick(all_dy, rows_dy, k, chip, columns[i])
            pl.when(k == chips - 1)(lambda i=i: first_parts(i))
        pl.when(k == 0)(loads[1].wait)

        def backs(j, total):
            at = pl.ds(pl.multiple_of(j * tile, tile), tile)
            up_at = pl.ds(pl.multiple_of(hidden + j * tile, tile), tile)
            back = lax.dot_general(rows_dy[k], w2[at, :], nt, preferred_element_type=F32)
            hid_grad = chance[:, 0:1] * back
            pg[k * 4 + rep, :, at] = (hid_grad * slope_up[:, at]).astype(BF16)
            pg[k * 4 + rep, :, up_at] = (hid_grad * act_keep[:, at]).astype(BF16)
            return total + jnp.sum(back * hid_keep[:, at].astype(F32), axis=1, keepdims=True)

        dprob = lax.fori_loop(0, hidden // tile, backs, jnp.zeros((rows, 1), F32))
        ret_p[k] = jnp.broadcast_to(dprob, (rows, 128)).T[0:16].astype(BF16)
        for i in range(2):
            grad_copy(k, i).start()

        def rows_back(j, carry):
            at = pl.ds(pl.multiple_of(j * tile, tile), tile)
            ret[k, :, at] = lax.dot_general(
                pg[k * 4 + rep], w1[at, :], nt, preferred_element_type=F32
            ).astype(BF16)
            return carry

        lax.fori_loop(0, width // tile, rows_back, 0)

        @pl.when(k == 0)
        def _():
            give_back(0)
            for c in keep_own():
                c.start()

        @pl.when(k == 2)
        def _():
            give_back(1)
            give_back(2)

        pl.when(k == 3)(lambda: give_back(3))
        return carry

    lax.fori_loop(0, chips, chunk, 0)

    def turn(k):
        for r in range(4):
            pl.when(r != rep)(lambda r=r: slice_wait(k, r))
            xs_t[:, (k * 4 + r) * rows : (k * 4 + r + 1) * rows] = xs[k * 4 + r].astype(F32).T.astype(BF16)

    early = 4 * (chips - 1)
    for k in range(chips - 1):
        turn(k)
        forward_wait(k)

    def sums(j, carry):
        at = pl.ds(pl.multiple_of(j * tile, tile), tile)
        g1_sum[:, at] = jnp.dot(
            xs_t[:, : early * rows], pg[0:early, :, at].reshape(early * rows, tile), preferred_element_type=F32
        )
        return carry

    lax.fori_loop(0, 2 * hidden // tile, sums, 0)
    for half in range(2):
        part_copy(half).wait_recv()
        mine = piece((rep_y, rep_x)[half], half)
        part_s[4 + half] = (mine + part_r[half].astype(F32)).astype(BF16)
        part_copy(4 + half).start()
    turn(chips - 1)

    named = tabs[me].astype(F32)
    owns = [placing(named, float(e))[0] for e in range(n)]
    for c in range(chips):
        own_t[:, c * 2 * cap : (c + 1) * 2 * cap] = (
            jnp.concatenate([owns[2 * c], owns[2 * c + 1]], axis=0).T.astype(BF16)
        )
    forward(chips - 1)
    for half in range(2):
        mine = piece(rep, half)
        part_copy(2 + half).wait_recv()
        part_copy(4 + half).wait_recv()
        g2_out[half * half_hidden : (half + 1) * half_hidden, :] = (
            mine + part_r[2 + half].astype(F32) + part_r[4 + half].astype(F32)
        ).astype(BF16)
    forward_wait(chips - 1)

    def finals(j, carry):
        at = pl.ds(pl.multiple_of(j * tile, tile), tile)
        last = pg[early : early + 4, :, at].reshape(4 * rows, tile)
        g1_out[:, at] = (
            g1_sum[:, at] + jnp.dot(xs_t[:, early * rows :], last, preferred_element_type=F32)
        ).astype(BF16)
        return carry

    lax.fori_loop(0, 2 * hidden // tile, finals, 0)

    for c in keep_own():
        c.wait()
    for e in range(n):

        @pl.when(e != me)
        def _(e=e):
            here = {"expert": e}
            send(ret_p.at[0], got_p.at[e], ret_send.at[0, 2], ret_recv.at[n + e], here).wait_recv()
            send(ret.at[0, pl.ds(0, cap)], got.at[e], ret_send.at[0, 0], ret_recv.at[e], here).wait_recv()

    def combine(j, carry):
        at = pl.ds(pl.multiple_of(j * tile, tile), tile)
        tok_out[:, at] = jnp.dot(
            own_t[...], got[:, :, at].reshape(n * cap, tile), preferred_element_type=F32
        ).astype(BF16)
        return carry

    lax.fori_loop(0, width // tile, combine, 0)
    found = [jnp.zeros((1, tok), F32)] * top
    odd = core.astype(F32)
    for e in range(n):
        spot = jnp.concatenate([owns[e] * (1.0 - odd), owns[e] * odd], axis=0).astype(BF16)
        value = jnp.dot(got_p[e], spot, preferred_element_type=F32)[0:1]
        found = [found[k] + jnp.where(named[k : k + 1] == float(e), value, 0.0) for k in range(top)]
    prob_out[...] = jnp.concatenate(found, axis=0).astype(BF16)

    for a in range(count):
        for way in range(3):
            guarded(ways[way][1], lambda a=a, way=way: along(a, me, None, way).wait_send())

    def drain(step, carry):
        for a in range(count):
            for hop, slot, here, way in hops(step):

                def one(a=a, hop=hop, slot=slot, way=way):
                    pl.when(ways[way][1])(lambda: along(a, slot, hop, way).wait_send())
                    along(a, slot, hop, 0).wait_send()

                pl.when(here)(one)
        return carry

    lax.fori_loop(1, chips, drain, 0)

    def drain_chunk(k, carry):
        for i in range(3):
            slice_copy(k, i).wait_send()
        for i in range(2):
            grad_copy(k, i).wait_send()
            forward_copy(k, i).wait_send()

            @pl.when(2 * chip_of(k) + i != me)
            def _(i=i):
                return_prob(k, i).wait_send()
                return_copy(k, i).wait_send()

        return carry

    lax.fori_loop(0, chips, drain_chunk, 0)
    for i in range(6):
        part_copy(i).wait_send()


def settle_kernel(*refs):
    count = len(refs) // 3
    ins, outs, held, sem = refs[:count], refs[count : 2 * count], refs[2 * count : 3 * count], refs[-1]
    takes = [pltpu.make_async_copy(ins[i], held[i], sem.at[0, i]) for i in range(count)]
    gives = [pltpu.make_async_copy(held[i], outs[i], sem.at[1, i]) for i in range(count)]
    for c in takes:
        c.start()
    for take, give in zip(takes, gives):
        take.wait()
        give.start()
    for c in gives:
        c.wait()


def settle(arrays):
    count = len(arrays)
    return pl.pallas_call(
        settle_kernel,
        out_shape=[jax.ShapeDtypeStruct(a.shape, a.dtype) for a in arrays],
        in_specs=[pl.BlockSpec(memory_space=pl.ANY)] * count,
        out_specs=[pl.BlockSpec(memory_space=pl.ANY)] * count,
        scratch_shapes=[pltpu.VMEM(a.shape, a.dtype) for a in arrays] + [pltpu.SemaphoreType.DMA((2, count))],
        compiler_params=pltpu.CompilerParams(vmem_limit_bytes=62 * 1024 * 1024),
    )(*arrays)


def fused(tokens, out_grad, routes, probs, w_one, w_two, n, cap):
    tok, width = tokens.shape
    top, hidden = routes.shape[1], w_two.shape[0]
    chips, rows, share = n // 2, 2 * cap, width // 4
    vmem, hbm = pl.BlockSpec(memory_space=pltpu.VMEM), pl.BlockSpec(memory_space=pl.ANY)
    dma = pltpu.SemaphoreType.DMA
    results = pl.pallas_call(
        lambda *refs: fused_kernel(top, *refs),
        out_shape=[
            jax.ShapeDtypeStruct((tok, width), BF16),
            jax.ShapeDtypeStruct((top, tok), BF16),
            jax.ShapeDtypeStruct((share, 2 * hidden), BF16),
            jax.ShapeDtypeStruct((hidden, share), BF16),
        ],
        in_specs=[vmem] * 2 + [hbm] * 4,
        out_specs=[vmem] * 4,
        scratch_shapes=[
            pltpu.VMEM((n, 16, tok), BF16),
            pltpu.VMEM((n, tok, width), BF16),
            pltpu.VMEM((n, tok, width), BF16),
            pltpu.VMEM((width, 2 * hidden), BF16),
            pltpu.VMEM((hidden, width), BF16),
            pltpu.VMEM((chips, rows, width), BF16),
            pltpu.VMEM((chips, rows, width), BF16),
            pltpu.VMEM((rows, 2 * tok), BF16),
            pltpu.VMEM((rows, 128), F32),
            pltpu.VMEM((rows, hidden), F32),
            pltpu.VMEM((rows, hidden), F32),
            pltpu.VMEM((rows, hidden), BF16),
            pltpu.VMEM((hidden, chips * rows), BF16),
            pltpu.VMEM((chips * 4, rows, 2 * hidden), BF16),
            pltpu.VMEM((chips * 4, rows, share), BF16),
            pltpu.VMEM((share, chips * 4 * rows), BF16),
            pltpu.VMEM((share, 2 * hidden), F32),
            pltpu.VMEM((chips, rows, width), BF16),
            pltpu.VMEM((chips, 16, rows), BF16),
            pltpu.VMEM((n, cap, width), BF16),
            pltpu.VMEM((n, 16, rows), BF16),
            pltpu.VMEM((tok, n * cap), BF16),
            pltpu.VMEM((6, hidden // 2, share), BF16),
            pltpu.VMEM((6, hidden // 2, share), BF16),
            dma((2,)),
            dma((2,)),
            dma((6, n - 1, 3)),
            dma((6, n)),
            dma((chips, 3)),
            dma((chips, 4)),
            dma((chips, 2)),
            dma((chips, 4)),
            dma((chips, 2)),
            dma((chips, 2)),
            dma((chips, 4)),
            dma((2 * n,)),
            dma((6,)),
            dma((6,)),
            dma((2,)),
        ],
        compiler_params=pltpu.CompilerParams(
            collective_id=0, has_side_effects=True, vmem_limit_bytes=62 * 1024 * 1024
        ),
    )(routes.T, probs.T, tokens, out_grad, w_one, w_two)
    token_grad, prob, share_one, share_two = settle(results)
    return token_grad, prob.T, share_one[None], share_two[None]


def swap(value, flip):
    return lax.ppermute(value, "dp", [(i, i ^ flip) for i in range(4)])


def square_first(piece):
    got = []
    for rest in (True, False):
        for half, side in ((0, 1), (1, 2)):
            flip = 3 if rest else side
            got.append(swap(piece(flip, half).astype(BF16), side))
    return got


def square_second(piece, got):
    sent = []
    for half, side in ((0, 2), (1, 1)):
        total = (piece(side, half) + got[half].astype(F32)).astype(BF16)
        sent.append(swap(total, side))
    return [
        (piece(0, half) + got[2 + half].astype(F32) + sent[half].astype(F32)).astype(BF16)
        for half in range(2)
    ]


def shards(tokens, out_grad, routes, probs, w_in, w_out):
    tok_rows, width = tokens.shape
    top = routes.shape[1]
    n_groups = lax.axis_size("expert")
    experts = n_groups * w_in.shape[0]
    hidden = w_out.shape[1]
    cap = 4 * tok_rows * top // (3 * experts)
    w_one, w_two = w_in[0], w_out[0]
    if n_groups == 8 and lax.axis_size("dp") == 4:
        return fused(tokens, out_grad, routes, probs, w_one, w_two, n_groups, cap)

    names = jnp.arange(experts, dtype=jnp.int32)
    named = routes[:, :, None] == names[None, None, :]
    hits = jnp.any(named, axis=1)
    later = (jnp.arange(tok_rows)[:, None] > jnp.arange(tok_rows)[None, :]).astype(BF16)
    rank = jnp.dot(later, hits.astype(BF16), preferred_element_type=F32)
    own_rank = jnp.sum(jnp.where(named, rank[:, None, :], 0.0), axis=2).astype(jnp.int32)
    slot = routes * cap + own_rank

    if experts <= 16:
        rows_x, rows_dy, rows_p, proj = dispatch_gather(tokens, out_grad, routes, probs, w_one, cap)
    else:
        rows_x, rows_dy, rows_p = dispatch_exchange(tokens, out_grad, probs, slot, experts, cap)
        proj = jnp.dot(rows_x, w_one, preferred_element_type=F32)
    rows_p = rows_p[:, None]
    gate, upper = proj[:, :hidden], proj[:, hidden:]
    sig = jax.nn.sigmoid(gate)
    act = gate * sig
    hid = (act * upper).astype(BF16)
    scaled = (rows_p * hid.astype(F32)).astype(BF16)
    replicas = lax.axis_size("dp")
    part = width // replicas
    at = lax.axis_index("dp")
    contract = (((0,), (0,)), ((), ()))

    def piece_two(flip, half):
        cut = lax.dynamic_slice_in_dim(rows_dy, (at ^ flip) * part, part, axis=1)
        units = scaled[:, half * (hidden // 2) : (half + 1) * (hidden // 2)]
        return lax.dot_general(units, cut, contract, preferred_element_type=F32)

    if replicas == 4:
        first_two = square_first(piece_two)
    else:
        grad_two = lax.dot_general(scaled, rows_dy, contract, preferred_element_type=F32).astype(BF16)
        share_two = lax.psum_scatter(grad_two, "dp", scatter_dimension=1, tiled=True)

    back = lax.dot_general(rows_dy, w_two, (((1,), (1,)), ((), ())), preferred_element_type=F32)
    dprob = jnp.sum(back * hid.astype(F32), axis=1).astype(BF16)
    hid_grad = rows_p * back
    proj_grad = jnp.concatenate(
        [hid_grad * upper * (sig * (1.0 + gate * (1.0 - sig))), hid_grad * act], axis=1
    ).astype(BF16)

    def piece_one(flip, half):
        cut = lax.dynamic_slice_in_dim(rows_x, (at ^ flip) * part, part, axis=1)
        units = proj_grad[:, half * hidden : (half + 1) * hidden]
        return lax.dot_general(cut, units, contract, preferred_element_type=F32)

    if replicas == 4:
        first_one = square_first(piece_one)
        second_two = square_second(piece_two, first_two)
        second_one = square_second(piece_one, first_one)
        share_two = jnp.concatenate(second_two, axis=0)
        share_one = jnp.concatenate(second_one, axis=1)
    else:
        grad_one = lax.dot_general(rows_x, proj_grad, contract, preferred_element_type=F32).astype(BF16)
        share_one = lax.psum_scatter(grad_one, "dp", scatter_dimension=0, tiled=True)

    row_grad = lax.dot_general(
        proj_grad, w_one, (((1,), (1,)), ((), ())), preferred_element_type=F32
    ).astype(BF16)
    back_x = lax.all_to_all(
        row_grad.reshape(n_groups, cap, width), "expert", split_axis=0, concat_axis=0, tiled=True
    ).reshape(experts * cap, width)
    back_p = lax.all_to_all(
        dprob.reshape(n_groups, cap), "expert", split_axis=0, concat_axis=0, tiled=True
    ).reshape(-1)
    slots = jnp.arange(experts * cap, dtype=jnp.int32)
    held = slot[:, :, None] == slots[None, None, :]
    prob_grad = jnp.sum(jnp.where(held, back_p.astype(F32), 0.0), axis=2).astype(BF16)
    token_grad = jnp.dot(
        jnp.any(held, axis=1).astype(BF16), back_x, preferred_element_type=F32
    ).astype(BF16)
    return token_grad, prob_grad, share_one[None], share_two[None]


def solution(mesh):
    return jax.shard_map(
        shards,
        mesh=mesh,
        in_specs=(
            P(("dp", "expert"), None),
            P(("dp", "expert"), None),
            P(("dp", "expert"), None),
            P(("dp", "expert"), None),
            P("expert", None, None),
            P("expert", None, None),
        ),
        out_specs=(
            P(("dp", "expert"), None),
            P(("dp", "expert"), None),
            P("expert", "dp", None),
            P("expert", None, "dp"),
        ),
        check_vma=False,
    )
```

```python
import jax
import jax.numpy as jnp
from jax import lax
from jax.experimental import pallas as pl
from jax.experimental.pallas import tpu as pltpu
from jax.sharding import PartitionSpec as P

F32 = jnp.float32
BF16 = jnp.bfloat16


def gather_kernel(n, cap, top, *refs):
    count = 3
    ins, w_hbm = refs[:count], refs[count]
    table_out, rows_x, rows_dy, proj = refs[count + 1 : count + 5]
    all_x, all_dy, w_vmem, w_sem, own_sem, send_sem, recv_sem = refs[count + 5 :]
    outs = (table_out, all_x, all_dy)
    load_w = pltpu.make_async_copy(w_hbm, w_vmem, w_sem)
    load_w.start()
    chips = n // 2
    me = lax.axis_index("expert")
    z, core = me // 2, me % 2
    ways = (
        (me - core + 1 - core, None),
        (me + 2, z < chips - 1),
        (me - 2, z > 0),
    )

    def guarded(ok, body):
        if ok is None:
            body()
        else:
            pl.when(ok)(body)

    barrier = pltpu.get_barrier_semaphore()
    for target, ok in ways:
        guarded(ok, lambda target=target: pl.semaphore_signal(
            barrier, inc=1, device_id={"expert": target}, device_id_type=pl.DeviceIdType.MESH
        ))
    peers = 1 + (z < chips - 1).astype(jnp.int32) + (z > 0).astype(jnp.int32)
    pl.semaphore_wait(barrier, peers)

    def copy(a, slot, hop, way):
        source = ins[a] if hop is None else outs[a].at[slot]
        return pltpu.make_async_remote_copy(
            src_ref=source,
            dst_ref=outs[a].at[slot],
            send_sem=send_sem.at[a, 0 if hop is None else hop, way],
            recv_sem=recv_sem.at[a, slot],
            device_id={"expert": ways[way][0]},
            device_id_type=pl.DeviceIdType.MESH,
        )

    def locals_():
        return [pltpu.make_async_copy(ins[a], outs[a].at[me], own_sem.at[a]) for a in range(count)]

    for c in locals_():
        c.start()
    hops = []
    for step in range(1, chips):
        hops.append((2 * step - 1, me - 2 * step, z - step >= 0, 1))
        hops.append((2 * step, me + 2 * step, z + step < chips, 2))
    def pick(rows_in, rows_out):
        tok = rows_in.shape[1]
        earlier = (
            lax.broadcasted_iota(jnp.int32, (tok, tok), 0) < lax.broadcasted_iota(jnp.int32, (tok, tok), 1)
        )
        earlier = jnp.where(earlier, 1.0, 0.0).astype(BF16)
        order = lax.broadcasted_iota(jnp.int32, (cap, tok), 0).astype(F32)

        def one(b, carry):
            named = table_out[b].astype(F32)
            hit = jnp.zeros((1, tok), F32)
            for k in range(top):
                hit = hit + jnp.where(named[k : k + 1] == me.astype(F32), 1.0, 0.0)
            rank = jnp.dot(
                jnp.broadcast_to(hit, (16, tok)).astype(BF16), earlier, preferred_element_type=F32
            )[0:1]
            place = jnp.where(order == rank, 1.0, 0.0) * hit
            rows_out[pl.ds(pl.multiple_of(b * cap, cap), cap), :] = jnp.dot(
                place.astype(BF16), rows_in[b], preferred_element_type=F32
            ).astype(BF16)
            return carry

        lax.fori_loop(0, n, one, 0)

    def send_own(a):
        for way in (1, 2, 0):
            guarded(ways[way][1], lambda a=a, way=way: copy(a, me, None, way).start())

    def pass_on(a):
        for hop, slot, here, way in hops:

            def relay(a=a, hop=hop, slot=slot, way=way):
                copy(a, slot, hop, way).wait_recv()
                pl.when(ways[way][1])(lambda: copy(a, slot, hop, way).start())
                copy(a, slot, hop, 0).start()

            pl.when(here)(relay)

    def finish(a):
        for chip in range(chips):
            copy(a, 2 * chip + 1 - core, 0, 0).wait_recv()

    send_own(0)
    send_own(1)
    pass_on(0)
    pass_on(1)
    send_own(2)
    for c in locals_():
        c.wait()
    finish(0)
    finish(1)
    load_w.wait()
    tile = 256
    steps = proj.shape[1] // tile
    width = steps // len(hops) if steps >= len(hops) else 0

    def columns(first, last):
        def one(i, carry):
            at = pl.ds(pl.multiple_of(i * tile, tile), tile)
            proj[:, at] = jnp.dot(rows_x[...], w_vmem[:, at], preferred_element_type=F32)
            return carry

        lax.fori_loop(first, last, one, 0)

    pick(all_x, rows_x)
    for i, (hop, slot, here, way) in enumerate(hops):

        def relay(hop=hop, slot=slot, way=way):
            copy(2, slot, hop, way).wait_recv()
            pl.when(ways[way][1])(lambda: copy(2, slot, hop, way).start())
            copy(2, slot, hop, 0).start()

        pl.when(here)(relay)
        columns(i * width, (i + 1) * width if i < len(hops) - 1 else steps)
    finish(2)
    pick(all_dy, rows_dy)
    for a in range(count):
        for way in range(3):
            guarded(ways[way][1], lambda a=a, way=way: copy(a, me, None, way).wait_send())
        for hop, slot, here, way in hops:

            def drain(a=a, hop=hop, slot=slot, way=way):
                pl.when(ways[way][1])(lambda: copy(a, slot, hop, way).wait_send())
                copy(a, slot, hop, 0).wait_send()

            pl.when(here)(drain)


def gather_all(n, cap, top, w_one, *arrays):
    table, rows = arrays[:2]
    vmem, width = pl.BlockSpec(memory_space=pltpu.VMEM), rows.shape[1]
    return pl.pallas_call(
        lambda *refs: gather_kernel(n, cap, top, *refs),
        out_shape=[
            jax.ShapeDtypeStruct((n,) + table.shape, BF16),
            jax.ShapeDtypeStruct((n * cap, width), BF16),
            jax.ShapeDtypeStruct((n * cap, width), BF16),
            jax.ShapeDtypeStruct((n * cap, w_one.shape[1]), F32),
        ],
        in_specs=[vmem] * 3 + [pl.BlockSpec(memory_space=pl.ANY)],
        out_specs=[vmem] * 4,
        scratch_shapes=[
            pltpu.VMEM((n,) + rows.shape, BF16),
            pltpu.VMEM((n,) + rows.shape, BF16),
            pltpu.VMEM(w_one.shape, BF16),
            pltpu.SemaphoreType.DMA,
            pltpu.SemaphoreType.DMA((3,)),
            pltpu.SemaphoreType.DMA((3, n - 1, 3)),
            pltpu.SemaphoreType.DMA((3, n)),
        ],
        compiler_params=pltpu.CompilerParams(
            collective_id=0, has_side_effects=True, vmem_limit_bytes=48 * 1024 * 1024
        ),
    )(*arrays, w_one)


def exclusive_rank(hits):
    rows = hits.shape[1]
    earlier = (jnp.arange(rows)[:, None] < jnp.arange(rows)[None, :]).astype(BF16)
    return jnp.dot(hits.astype(BF16), earlier, preferred_element_type=F32)


def dispatch_gather(tokens, out_grad, routes, probs, w_one, cap):
    tok_rows, width = tokens.shape
    top = routes.shape[1]
    me = lax.axis_index("expert").astype(F32)
    table = jnp.concatenate([routes.T.astype(BF16), probs.T], axis=0)
    table = jnp.pad(table, ((0, -2 * top % 16), (0, 0)))
    table, rows_x, rows_dy, proj = gather_all(
        lax.axis_size("expert"), cap, top, w_one, table, tokens, out_grad
    )
    table = table.astype(F32)
    mine = table[:, :top] == me
    hits = jnp.any(mine, axis=1)
    prob = jnp.sum(jnp.where(mine, table[:, top : 2 * top], 0.0), axis=1)
    rank = exclusive_rank(hits)
    place = (rank[:, None, :] == jnp.arange(cap, dtype=F32)[None, :, None]) & hits[:, None, :]
    rows_p = jnp.sum(jnp.where(place, prob[:, None, :], 0.0), axis=2).reshape(-1)
    return rows_x, rows_dy, rows_p, proj


def dispatch_exchange(tokens, out_grad, probs, slot, experts, cap):
    tok_rows, width = tokens.shape
    top = slot.shape[1]
    flat = slot.reshape(-1)
    slot_hit = flat[:, None] == jnp.arange(experts * cap, dtype=jnp.int32)[None, :]
    filled = jnp.any(slot_hit, axis=0)
    owner = jnp.sum(jnp.where(slot_hit, jnp.arange(flat.shape[0], dtype=jnp.int32)[:, None], 0), axis=0)
    source = owner // top
    zero = jnp.zeros((), BF16)

    def move(rows):
        return lax.all_to_all(rows, "expert", split_axis=0, concat_axis=0, tiled=True)

    send_x = jnp.where(filled[:, None], tokens[source], zero).reshape(experts, cap, width)
    send_dy = jnp.where(filled[:, None], out_grad[source], zero).reshape(experts, cap, width)
    send_p = jnp.where(filled, probs.reshape(-1)[owner], zero).reshape(experts, cap)
    return (
        move(send_x).reshape(-1, width),
        move(send_dy).reshape(-1, width),
        move(send_p).reshape(-1).astype(F32),
    )


def fused_kernel(top, *refs):
    routes_in, probs_in, x_hbm, dy_hbm, w1_hbm, w2_hbm = refs[:6]
    outputs = refs[6:10]
    tabs, all_x, all_dy, w1, w2, rows_x, rows_dy, places, chance = refs[10:19]
    slope_up, act_keep, hid_keep, hid_t, pg, xs, xs_t, g1_sum = refs[19:27]
    ret, ret_p, got, got_p, own_t, part_s, part_r = refs[27:34]
    own_sem, w_sem, z_send, z_recv, xs_send, xs_recv, pg_send, pg_recv = refs[34:42]
    fw_send, fw_recv, ret_send, ret_recv, part_send, part_recv, keep_sem = refs[42:49]
    back_sum, tok_out, prob_out, g1_out, g2_out, out_sem, g1_sem = refs[49:]
    count = 6
    n, tok, width = all_x.shape
    rows = rows_x.shape[1]
    cap = rows // 2
    hidden = w2.shape[0]
    share = width // 4
    half_hidden = hidden // 2
    chips = n // 2
    me, rep = lax.axis_index("expert"), lax.axis_index("dp")
    z, core = me // 2, me % 2
    rep_x = rep + 1 - 2 * (rep % 2)
    rep_y = rep + 2 - 4 * (rep // 2)
    rep_d = 3 - rep
    tile = 256

    barrier = pltpu.get_barrier_semaphore()
    for i in range(1, n):
        pl.semaphore_signal(
            barrier, inc=1, device_id={"expert": (me + i) % n}, device_id_type=pl.DeviceIdType.MESH
        )
    for target in (rep_x, rep_y, rep_d):
        pl.semaphore_signal(
            barrier, inc=1, device_id={"dp": target}, device_id_type=pl.DeviceIdType.MESH
        )

    columns = (rep_d, rep_x, rep_y, rep)

    def quarter(i):
        return pl.ds(pl.multiple_of(columns[i] * share, share), share)

    def own(a):
        return (tabs.at[me], x_hbm)[a] if a < 2 else dy_hbm.at[:, quarter(a - 2)]

    def held(a, slot):
        return (tabs, all_x)[a].at[slot] if a < 2 else all_dy.at[slot, :, quarter(a - 2)]

    loads = [pltpu.make_async_copy(w1_hbm, w1, w_sem.at[0]), pltpu.make_async_copy(w2_hbm, w2, w_sem.at[1])]
    keeps = [
        pltpu.make_async_copy(x_hbm, all_x.at[me], own_sem.at[0]),
        pltpu.make_async_copy(dy_hbm, all_dy.at[me], own_sem.at[1]),
    ]
    for c in keeps + loads:
        c.start()
    tabs[me] = jnp.concatenate(
        [routes_in[...].astype(F32), probs_in[...].astype(F32), jnp.zeros((16 - 2 * top, tok), F32)], axis=0
    ).astype(BF16)

    pl.semaphore_wait(barrier, n - 1 + 3)

    ways = ((me - core + 1 - core, None), (me + 2, z < chips - 1), (me - 2, z > 0))

    def guarded(ok, body):
        if ok is None:
            body()
        else:
            pl.when(ok)(body)

    def send(src, dst, send_sem, recv_sem, device):
        return pltpu.make_async_remote_copy(
            src_ref=src,
            dst_ref=dst,
            send_sem=send_sem,
            recv_sem=recv_sem,
            device_id=device,
            device_id_type=pl.DeviceIdType.MESH,
        )

    def along(a, slot, hop, way):
        source = own(a) if hop is None else held(a, slot)
        return send(
            source,
            held(a, slot),
            z_send.at[a, 0 if hop is None else hop, way],
            z_recv.at[a, slot],
            {"expert": ways[way][0]},
        )

    def hops(step):
        return (
            (2 * step - 1, me - 2 * step, z - step >= 0, 1),
            (2 * step, me + 2 * step, z + step < chips, 2),
        )

    def pass_on(a, step):
        for hop, slot, here, way in hops(step):

            def relay(hop=hop, slot=slot, way=way):
                along(a, slot, hop, way).wait_recv()
                pl.when(ways[way][1])(lambda: along(a, slot, hop, way).start())
                along(a, slot, hop, 0).start()

            pl.when(here)(relay)

    def chip_of(k):
        upper = z // 2
        low = z + upper * (3 - 2 * z)
        near = k + low * (1 - k // 2) * (1 - 2 * k)
        return near + upper * (3 - 2 * near)

    def slice_copy(k, i):
        target = (rep_x, rep_y, rep_d)[i]
        return send(
            rows_x.at[k, :, pl.ds(pl.multiple_of(target * share, share), share)],
            xs.at[k * 4 + rep],
            xs_send.at[k, i],
            xs_recv.at[k, rep],
            {"dp": target},
        )

    def slice_wait(k, other):
        send(
            rows_x.at[k, :, pl.ds(0, share)], xs.at[k * 4 + other], xs_send.at[k, 0], xs_recv.at[k, other], {"dp": other}
        ).wait_recv()

    def grad_copy(k, i):
        return send(
            pg.at[k * 4 + rep], pg.at[k * 4 + rep], pg_send.at[k, i], pg_recv.at[k, rep], {"dp": (rep_x, rep_y)[i]}
        )

    def grad_wait(k, other):
        send(pg.at[k * 4 + other], pg.at[k * 4 + other], pg_send.at[k, 0], pg_recv.at[k, other], {"dp": other}).wait_recv()

    def forward_copy(k, i):
        came, goes = ((rep_x, rep_y), (rep_y, rep_x))[i]
        part = pg.at[k * 4 + came, pl.ds(i * cap, cap)]
        return send(part, part, fw_send.at[k, i], fw_recv.at[k, i], {"dp": goes})

    def forward_wait(k):
        for i in range(2):
            part = pg.at[k * 4 + rep_d, pl.ds(i * cap, cap)]
            send(part, part, fw_send.at[k, i], fw_recv.at[k, i], {"dp": (rep_y, rep_x)[i]}).wait_recv()

    def forward(k):
        grad_wait(k, rep_x)
        forward_copy(k, 0).start()
        grad_wait(k, rep_y)
        forward_copy(k, 1).start()

    def return_copy(k, i):
        return send(
            ret.at[k, pl.ds(i * cap, cap)],
            got.at[me],
            ret_send.at[k, i],
            ret_recv.at[me],
            {"expert": 2 * chip_of(k) + i},
        )

    def return_prob(k, i):
        return send(
            ret_p.at[k], got_p.at[me], ret_send.at[k, 2 + i], ret_recv.at[n + me], {"expert": 2 * chip_of(k) + i}
        )

    def give_back(k):
        for i in range(2):

            @pl.when(2 * chip_of(k) + i != me)
            def _(i=i):
                return_prob(k, i).start()
                return_copy(k, i).start()

    def keep_own():
        return [
            pltpu.make_async_copy(ret.at[0, pl.ds(core * cap, cap)], got.at[me], keep_sem.at[0]),
            pltpu.make_async_copy(ret_p.at[0], got_p.at[me], keep_sem.at[1]),
        ]

    def piece(column, half):
        dy = rows_dy[:, :, pl.ds(pl.multiple_of(column * share, share), share)].reshape(chips * rows, share)
        return jnp.dot(
            hid_t[half * half_hidden : (half + 1) * half_hidden], dy, preferred_element_type=F32
        )

    sides = (rep_x, rep_y, rep_x, rep_y, rep_y, rep_x)

    def part_copy(i):
        return send(part_s.at[i], part_r.at[i], part_send.at[i], part_recv.at[i], {"dp": sides[i]})

    def first_parts(i):
        for slot in ((0, 1), (2,), (3,), ())[i]:
            part_s[slot] = piece(columns[i], slot % 2).astype(BF16)
            part_copy(slot).start()

    for a in range(count):
        for way in (1, 2, 0):
            guarded(ways[way][1], lambda a=a, way=way: along(a, me, None, way).start())

    earlier = lax.broadcasted_iota(jnp.int32, (tok, tok), 0) < lax.broadcasted_iota(jnp.int32, (tok, tok), 1)
    earlier = jnp.where(earlier, 1.0, 0.0).astype(BF16)
    order = lax.broadcasted_iota(jnp.int32, (cap, tok), 0).astype(F32)

    def placing(named, expert):
        hit = jnp.zeros((1, tok), F32)
        prob = jnp.zeros((1, tok), F32)
        for k in range(top):
            match = jnp.where(named[k : k + 1] == expert, 1.0, 0.0)
            hit = hit + match
            prob = prob + match * named[top + k : top + k + 1]
        rank = jnp.dot(
            jnp.broadcast_to(hit, (16, tok)).astype(BF16), earlier, preferred_element_type=F32
        )[0:1]
        return jnp.where(order == rank, 1.0, 0.0) * hit, prob

    nt = (((1,), (1,)), ((), ()))

    def pick(source, target, k, chip, column):
        at = pl.ds(pl.multiple_of(column * share, share), share)
        pair = source[pl.ds(2 * chip, 2), :, at].reshape(2 * tok, share)
        target[k, :, at] = jnp.dot(places[...], pair, preferred_element_type=F32).astype(BF16)

    def chunk(k, carry):
        chip = chip_of(k)
        other = 2 * chip + 1 - core

        def relays(a):
            pl.when(k > 0)(lambda: pass_on(a, k))
            if a in (1, 2):
                pl.when(k == 0)(keeps[a - 1].wait)
            along(a, other, 0, 0).wait_recv()

        relays(0)
        relays(1)
        blocks, probs = [], []
        blank = jnp.zeros((cap, tok), F32)
        for i in range(2):
            place, prob = placing(tabs[2 * chip + i].astype(F32), me.astype(F32))
            blocks.append(jnp.concatenate([blank] * i + [place] + [blank] * (1 - i), axis=1))
            probs.append(jnp.sum(place * prob, axis=1, keepdims=True))
        places[...] = jnp.concatenate(blocks, axis=0).astype(BF16)
        chance[...] = jnp.broadcast_to(jnp.concatenate(probs, axis=0), chance.shape)
        for i in range(4):
            pick(all_x, rows_x, k, chip, i)
        for i in range(3):
            slice_copy(k, i).start()
        xs[k * 4 + rep] = rows_x[k, :, pl.ds(pl.multiple_of(rep * share, share), share)]
        pl.when(k == 0)(loads[0].wait)

        def units(j, carry):
            at = pl.ds(pl.multiple_of(j * tile, tile), tile)
            up_at = pl.ds(pl.multiple_of(hidden + j * tile, tile), tile)
            gate = jnp.dot(rows_x[k], w1[:, at], preferred_element_type=F32)
            upper = jnp.dot(rows_x[k], w1[:, up_at], preferred_element_type=F32)
            sig = jax.nn.sigmoid(gate)
            act = gate * sig
            hid = (act * upper).astype(BF16)
            scaled = chance[:, 0:1] * hid.astype(F32)
            slope_up[:, at] = upper * (sig * (1.0 + gate * (1.0 - sig)))
            act_keep[:, at] = act
            hid_keep[:, at] = hid
            hid_t[at, pl.ds(pl.multiple_of(k * rows, rows), rows)] = scaled.T.astype(BF16)
            return carry

        lax.fori_loop(0, hidden // tile, units, 0)
        pl.when(k > 0)(lambda: forward(k - 1))
        for i in range(4):
            relays(2 + i)
            pick(all_dy, rows_dy, k, chip, columns[i])
            pl.when(k == chips - 1)(lambda i=i: first_parts(i))
            if i == 0:
                pl.when(k == 0)(loads[1].wait)
            gained = lax.dot_general(
                rows_dy[k, :, quarter(i)], w2[:, quarter(i)], nt, preferred_element_type=F32
            )
            back_sum[...] = gained if i == 0 else back_sum[...] + gained

        def backs(j, total):
            at = pl.ds(pl.multiple_of(j * tile, tile), tile)
            up_at = pl.ds(pl.multiple_of(hidden + j * tile, tile), tile)
            back = back_sum[:, at]
            hid_grad = chance[:, 0:1] * back
            pg[k * 4 + rep, :, at] = (hid_grad * slope_up[:, at]).astype(BF16)
            pg[k * 4 + rep, :, up_at] = (hid_grad * act_keep[:, at]).astype(BF16)
            return total + jnp.sum(back * hid_keep[:, at].astype(F32), axis=1, keepdims=True)

        dprob = lax.fori_loop(0, hidden // tile, backs, jnp.zeros((rows, 1), F32))
        ret_p[k] = jnp.broadcast_to(dprob, (rows, 128)).T[0:16].astype(BF16)
        for i in range(2):
            grad_copy(k, i).start()

        def rows_back(j, carry):
            at = pl.ds(pl.multiple_of(j * tile, tile), tile)
            ret[k, :, at] = lax.dot_general(
                pg[k * 4 + rep], w1[at, :], nt, preferred_element_type=F32
            ).astype(BF16)
            return carry

        lax.fori_loop(0, width // tile, rows_back, 0)

        @pl.when(k == 0)
        def _():
            give_back(0)
            for c in keep_own():
                c.start()

        @pl.when(k == 2)
        def _():
            give_back(1)
            give_back(2)

        pl.when(k == 3)(lambda: give_back(3))
        return carry

    lax.fori_loop(0, chips, chunk, 0)

    origin = (rep, rep_x, rep_y, rep_d)

    def turn(k):
        for p in range(4):
            if p:
                slice_wait(k, origin[p])
            at = k * 4 + p
            xs_t[:, at * rows : (at + 1) * rows] = xs[k * 4 + origin[p]].astype(F32).T.astype(BF16)

    def gathered(k, at, first, last):
        return [pg[k * 4 + origin[p], :, at] for p in range(first, last)]

    early = 4 * (chips - 1)
    for k in range(chips - 1):
        turn(k)
        forward_wait(k)

    def sums(j, carry):
        at = pl.ds(pl.multiple_of(j * tile, tile), tile)
        parts = [part for k in range(chips - 1) for part in gathered(k, at, 0, 4)]
        g1_sum[:, at] = jnp.dot(
            xs_t[:, : early * rows], jnp.concatenate(parts, axis=0), preferred_element_type=F32
        )
        return carry

    lax.fori_loop(0, 2 * hidden // tile, sums, 0)
    for half in range(2):
        part_copy(half).wait_recv()
        mine = piece((rep_y, rep_x)[half], half)
        part_s[4 + half] = (mine + part_r[half].astype(F32)).astype(BF16)
        part_copy(4 + half).start()
    turn(chips - 1)

    named = tabs[me].astype(F32)
    owns = [placing(named, float(e))[0] for e in range(n)]
    for c in range(chips):
        own_t[:, c * 2 * cap : (c + 1) * 2 * cap] = (
            jnp.concatenate([owns[2 * c], owns[2 * c + 1]], axis=0).T.astype(BF16)
        )
    forward(chips - 1)

    def near(j, carry):
        at = pl.ds(pl.multiple_of(j * tile, tile), tile)
        g1_sum[:, at] = g1_sum[:, at] + jnp.dot(
            xs_t[:, early * rows : (early + 3) * rows],
            jnp.concatenate(gathered(chips - 1, at, 0, 3), axis=0),
            preferred_element_type=F32,
        )
        return carry

    lax.fori_loop(0, 2 * hidden // tile, near, 0)
    writes = [
        pltpu.make_async_copy(ref, outputs[i], out_sem.at[i])
        for i, ref in ((0, tok_out), (1, prob_out), (3, g2_out))
    ]
    for half in range(2):
        mine = piece(rep, half)
        part_copy(2 + half).wait_recv()
        part_copy(4 + half).wait_recv()
        g2_out[half * half_hidden : (half + 1) * half_hidden, :] = (
            mine + part_r[2 + half].astype(F32) + part_r[4 + half].astype(F32)
        ).astype(BF16)
    writes[2].start()

    for c in keep_own():
        c.wait()
    for e in range(n):

        @pl.when(e != me)
        def _(e=e):
            here = {"expert": e}
            send(ret_p.at[0], got_p.at[e], ret_send.at[0, 2], ret_recv.at[n + e], here).wait_recv()
            send(ret.at[0, pl.ds(0, cap)], got.at[e], ret_send.at[0, 0], ret_recv.at[e], here).wait_recv()

    def combine(j, carry):
        at = pl.ds(pl.multiple_of(j * tile, tile), tile)
        tok_out[:, at] = jnp.dot(
            own_t[...], got[:, :, at].reshape(n * cap, tile), preferred_element_type=F32
        ).astype(BF16)
        return carry

    lax.fori_loop(0, width // tile, combine, 0)
    writes[0].start()
    found = [jnp.zeros((1, tok), F32)] * top
    odd = core.astype(F32)
    for e in range(n):
        spot = jnp.concatenate([owns[e] * (1.0 - odd), owns[e] * odd], axis=0).astype(BF16)
        value = jnp.dot(got_p[e], spot, preferred_element_type=F32)[0:1]
        found = [found[k] + jnp.where(named[k : k + 1] == float(e), value, 0.0) for k in range(top)]
    prob_out[...] = jnp.concatenate(found, axis=0).astype(BF16)
    writes[1].start()
    forward_wait(chips - 1)

    def put(j):
        at = pl.ds(pl.multiple_of(j * tile, tile), tile)
        return pltpu.make_async_copy(g1_out.at[:, at], outputs[2].at[:, at], g1_sem.at[j])

    def finals(j, carry):
        at = pl.ds(pl.multiple_of(j * tile, tile), tile)
        g1_out[:, at] = (
            g1_sum[:, at]
            + jnp.dot(xs_t[:, (early + 3) * rows :], pg[early + rep_d, :, at], preferred_element_type=F32)
        ).astype(BF16)
        put(j).start()
        return carry

    lax.fori_loop(0, 2 * hidden // tile, finals, 0)

    for a in range(count):
        for way in range(3):
            guarded(ways[way][1], lambda a=a, way=way: along(a, me, None, way).wait_send())

    def drain(step, carry):
        for a in range(count):
            for hop, slot, here, way in hops(step):

                def one(a=a, hop=hop, slot=slot, way=way):
                    pl.when(ways[way][1])(lambda: along(a, slot, hop, way).wait_send())
                    along(a, slot, hop, 0).wait_send()

                pl.when(here)(one)
        return carry

    lax.fori_loop(1, chips, drain, 0)

    def drain_chunk(k, carry):
        for i in range(3):
            slice_copy(k, i).wait_send()
        for i in range(2):
            grad_copy(k, i).wait_send()
            forward_copy(k, i).wait_send()

            @pl.when(2 * chip_of(k) + i != me)
            def _(i=i):
                return_prob(k, i).wait_send()
                return_copy(k, i).wait_send()

        return carry

    lax.fori_loop(0, chips, drain_chunk, 0)
    for i in range(6):
        part_copy(i).wait_send()
    for c in writes:
        c.wait()
    for j in range(2 * hidden // tile):
        put(j).wait()


def settle_kernel(*refs):
    count = len(refs) // 3
    ins, outs, held, sem = refs[:count], refs[count : 2 * count], refs[2 * count : 3 * count], refs[-1]
    takes = [pltpu.make_async_copy(ins[i], held[i], sem.at[0, i]) for i in range(count)]
    gives = [pltpu.make_async_copy(held[i], outs[i], sem.at[1, i]) for i in range(count)]
    for c in takes:
        c.start()
    for take, give in zip(takes, gives):
        take.wait()
        give.start()
    for c in gives:
        c.wait()


def settle(arrays):
    count = len(arrays)
    return pl.pallas_call(
        settle_kernel,
        out_shape=[jax.ShapeDtypeStruct(a.shape, a.dtype) for a in arrays],
        in_specs=[pl.BlockSpec(memory_space=pl.ANY)] * count,
        out_specs=[pl.BlockSpec(memory_space=pl.ANY)] * count,
        scratch_shapes=[pltpu.VMEM(a.shape, a.dtype) for a in arrays] + [pltpu.SemaphoreType.DMA((2, count))],
        compiler_params=pltpu.CompilerParams(vmem_limit_bytes=62 * 1024 * 1024),
    )(*arrays)


def fused(tokens, out_grad, routes, probs, w_one, w_two, n, cap):
    tok, width = tokens.shape
    top, hidden = routes.shape[1], w_two.shape[0]
    chips, rows, share = n // 2, 2 * cap, width // 4
    vmem, hbm = pl.BlockSpec(memory_space=pltpu.VMEM), pl.BlockSpec(memory_space=pl.ANY)
    dma = pltpu.SemaphoreType.DMA
    results = pl.pallas_call(
        lambda *refs: fused_kernel(top, *refs),
        out_shape=[
            jax.ShapeDtypeStruct((tok, width), BF16),
            jax.ShapeDtypeStruct((top, tok), BF16),
            jax.ShapeDtypeStruct((share, 2 * hidden), BF16),
            jax.ShapeDtypeStruct((hidden, share), BF16),
        ],
        in_specs=[vmem] * 2 + [hbm] * 4,
        out_specs=[hbm] * 4,
        scratch_shapes=[
            pltpu.VMEM((n, 16, tok), BF16),
            pltpu.VMEM((n, tok, width), BF16),
            pltpu.VMEM((n, tok, width), BF16),
            pltpu.VMEM((width, 2 * hidden), BF16),
            pltpu.VMEM((hidden, width), BF16),
            pltpu.VMEM((chips, rows, width), BF16),
            pltpu.VMEM((chips, rows, width), BF16),
            pltpu.VMEM((rows, 2 * tok), BF16),
            pltpu.VMEM((rows, 128), F32),
            pltpu.VMEM((rows, hidden), F32),
            pltpu.VMEM((rows, hidden), F32),
            pltpu.VMEM((rows, hidden), BF16),
            pltpu.VMEM((hidden, chips * rows), BF16),
            pltpu.VMEM((chips * 4, rows, 2 * hidden), BF16),
            pltpu.VMEM((chips * 4, rows, share), BF16),
            pltpu.VMEM((share, chips * 4 * rows), BF16),
            pltpu.VMEM((share, 2 * hidden), F32),
            pltpu.VMEM((chips, rows, width), BF16),
            pltpu.VMEM((chips, 16, rows), BF16),
            pltpu.VMEM((n, cap, width), BF16),
            pltpu.VMEM((n, 16, rows), BF16),
            pltpu.VMEM((tok, n * cap), BF16),
            pltpu.VMEM((6, hidden // 2, share), BF16),
            pltpu.VMEM((6, hidden // 2, share), BF16),
            dma((2,)),
            dma((2,)),
            dma((6, n - 1, 3)),
            dma((6, n)),
            dma((chips, 3)),
            dma((chips, 4)),
            dma((chips, 2)),
            dma((chips, 4)),
            dma((chips, 2)),
            dma((chips, 2)),
            dma((chips, 4)),
            dma((2 * n,)),
            dma((6,)),
            dma((6,)),
            dma((2,)),
            pltpu.VMEM((rows, hidden), F32),
            pltpu.VMEM((tok, width), BF16),
            pltpu.VMEM((top, tok), BF16),
            pltpu.VMEM((share, 2 * hidden), BF16),
            pltpu.VMEM((hidden, share), BF16),
            dma((4,)),
            dma((2 * hidden // 256,)),
        ],
        compiler_params=pltpu.CompilerParams(
            collective_id=0, has_side_effects=True, vmem_limit_bytes=62 * 1024 * 1024
        ),
    )(routes.T, probs.T, tokens, out_grad, w_one, w_two)
    token_grad, prob, share_one, share_two = settle(results)
    return token_grad, prob.T, share_one[None], share_two[None]


def swap(value, flip):
    return lax.ppermute(value, "dp", [(i, i ^ flip) for i in range(4)])


def square_first(piece):
    got = []
    for rest in (True, False):
        for half, side in ((0, 1), (1, 2)):
            flip = 3 if rest else side
            got.append(swap(piece(flip, half).astype(BF16), side))
    return got


def square_second(piece, got):
    sent = []
    for half, side in ((0, 2), (1, 1)):
        total = (piece(side, half) + got[half].astype(F32)).astype(BF16)
        sent.append(swap(total, side))
    return [
        (piece(0, half) + got[2 + half].astype(F32) + sent[half].astype(F32)).astype(BF16)
        for half in range(2)
    ]


def shards(tokens, out_grad, routes, probs, w_in, w_out):
    tok_rows, width = tokens.shape
    top = routes.shape[1]
    n_groups = lax.axis_size("expert")
    experts = n_groups * w_in.shape[0]
    hidden = w_out.shape[1]
    cap = 4 * tok_rows * top // (3 * experts)
    w_one, w_two = w_in[0], w_out[0]
    if n_groups == 8 and lax.axis_size("dp") == 4:
        return fused(tokens, out_grad, routes, probs, w_one, w_two, n_groups, cap)

    names = jnp.arange(experts, dtype=jnp.int32)
    named = routes[:, :, None] == names[None, None, :]
    hits = jnp.any(named, axis=1)
    later = (jnp.arange(tok_rows)[:, None] > jnp.arange(tok_rows)[None, :]).astype(BF16)
    rank = jnp.dot(later, hits.astype(BF16), preferred_element_type=F32)
    own_rank = jnp.sum(jnp.where(named, rank[:, None, :], 0.0), axis=2).astype(jnp.int32)
    slot = routes * cap + own_rank

    if experts <= 16:
        rows_x, rows_dy, rows_p, proj = dispatch_gather(tokens, out_grad, routes, probs, w_one, cap)
    else:
        rows_x, rows_dy, rows_p = dispatch_exchange(tokens, out_grad, probs, slot, experts, cap)
        proj = jnp.dot(rows_x, w_one, preferred_element_type=F32)
    rows_p = rows_p[:, None]
    gate, upper = proj[:, :hidden], proj[:, hidden:]
    sig = jax.nn.sigmoid(gate)
    act = gate * sig
    hid = (act * upper).astype(BF16)
    scaled = (rows_p * hid.astype(F32)).astype(BF16)
    replicas = lax.axis_size("dp")
    part = width // replicas
    at = lax.axis_index("dp")
    contract = (((0,), (0,)), ((), ()))

    def piece_two(flip, half):
        cut = lax.dynamic_slice_in_dim(rows_dy, (at ^ flip) * part, part, axis=1)
        units = scaled[:, half * (hidden // 2) : (half + 1) * (hidden // 2)]
        return lax.dot_general(units, cut, contract, preferred_element_type=F32)

    if replicas == 4:
        first_two = square_first(piece_two)
    else:
        grad_two = lax.dot_general(scaled, rows_dy, contract, preferred_element_type=F32).astype(BF16)
        share_two = lax.psum_scatter(grad_two, "dp", scatter_dimension=1, tiled=True)

    back = lax.dot_general(rows_dy, w_two, (((1,), (1,)), ((), ())), preferred_element_type=F32)
    dprob = jnp.sum(back * hid.astype(F32), axis=1).astype(BF16)
    hid_grad = rows_p * back
    proj_grad = jnp.concatenate(
        [hid_grad * upper * (sig * (1.0 + gate * (1.0 - sig))), hid_grad * act], axis=1
    ).astype(BF16)

    def piece_one(flip, half):
        cut = lax.dynamic_slice_in_dim(rows_x, (at ^ flip) * part, part, axis=1)
        units = proj_grad[:, half * hidden : (half + 1) * hidden]
        return lax.dot_general(cut, units, contract, preferred_element_type=F32)

    if replicas == 4:
        first_one = square_first(piece_one)
        second_two = square_second(piece_two, first_two)
        second_one = square_second(piece_one, first_one)
        share_two = jnp.concatenate(second_two, axis=0)
        share_one = jnp.concatenate(second_one, axis=1)
    else:
        grad_one = lax.dot_general(rows_x, proj_grad, contract, preferred_element_type=F32).astype(BF16)
        share_one = lax.psum_scatter(grad_one, "dp", scatter_dimension=0, tiled=True)

    row_grad = lax.dot_general(
        proj_grad, w_one, (((1,), (1,)), ((), ())), preferred_element_type=F32
    ).astype(BF16)
    back_x = lax.all_to_all(
        row_grad.reshape(n_groups, cap, width), "expert", split_axis=0, concat_axis=0, tiled=True
    ).reshape(experts * cap, width)
    back_p = lax.all_to_all(
        dprob.reshape(n_groups, cap), "expert", split_axis=0, concat_axis=0, tiled=True
    ).reshape(-1)
    slots = jnp.arange(experts * cap, dtype=jnp.int32)
    held = slot[:, :, None] == slots[None, None, :]
    prob_grad = jnp.sum(jnp.where(held, back_p.astype(F32), 0.0), axis=2).astype(BF16)
    token_grad = jnp.dot(
        jnp.any(held, axis=1).astype(BF16), back_x, preferred_element_type=F32
    ).astype(BF16)
    return token_grad, prob_grad, share_one[None], share_two[None]


def solution(mesh):
    return jax.shard_map(
        shards,
        mesh=mesh,
        in_specs=(
            P(("dp", "expert"), None),
            P(("dp", "expert"), None),
            P(("dp", "expert"), None),
            P(("dp", "expert"), None),
            P("expert", None, None),
            P("expert", None, None),
        ),
        out_specs=(
            P(("dp", "expert"), None),
            P(("dp", "expert"), None),
            P("expert", "dp", None),
            P("expert", None, "dp"),
        ),
        check_vma=False,
    )
```

```python
import jax
import jax.numpy as jnp
from jax import lax
from jax.experimental import pallas as pl
from jax.experimental.pallas import tpu as pltpu
from jax.sharding import PartitionSpec as P

F32 = jnp.float32
BF16 = jnp.bfloat16


def gather_kernel(n, cap, top, *refs):
    count = 3
    ins, w_hbm = refs[:count], refs[count]
    table_out, rows_x, rows_dy, proj = refs[count + 1 : count + 5]
    all_x, all_dy, w_vmem, w_sem, own_sem, send_sem, recv_sem = refs[count + 5 :]
    outs = (table_out, all_x, all_dy)
    load_w = pltpu.make_async_copy(w_hbm, w_vmem, w_sem)
    load_w.start()
    chips = n // 2
    me = lax.axis_index("expert")
    z, core = me // 2, me % 2
    ways = (
        (me - core + 1 - core, None),
        (me + 2, z < chips - 1),
        (me - 2, z > 0),
    )

    def guarded(ok, body):
        if ok is None:
            body()
        else:
            pl.when(ok)(body)

    barrier = pltpu.get_barrier_semaphore()
    for target, ok in ways:
        guarded(ok, lambda target=target: pl.semaphore_signal(
            barrier, inc=1, device_id={"expert": target}, device_id_type=pl.DeviceIdType.MESH
        ))
    peers = 1 + (z < chips - 1).astype(jnp.int32) + (z > 0).astype(jnp.int32)
    pl.semaphore_wait(barrier, peers)

    def copy(a, slot, hop, way):
        source = ins[a] if hop is None else outs[a].at[slot]
        return pltpu.make_async_remote_copy(
            src_ref=source,
            dst_ref=outs[a].at[slot],
            send_sem=send_sem.at[a, 0 if hop is None else hop, way],
            recv_sem=recv_sem.at[a, slot],
            device_id={"expert": ways[way][0]},
            device_id_type=pl.DeviceIdType.MESH,
        )

    def locals_():
        return [pltpu.make_async_copy(ins[a], outs[a].at[me], own_sem.at[a]) for a in range(count)]

    for c in locals_():
        c.start()
    hops = []
    for step in range(1, chips):
        hops.append((2 * step - 1, me - 2 * step, z - step >= 0, 1))
        hops.append((2 * step, me + 2 * step, z + step < chips, 2))
    def pick(rows_in, rows_out):
        tok = rows_in.shape[1]
        earlier = (
            lax.broadcasted_iota(jnp.int32, (tok, tok), 0) < lax.broadcasted_iota(jnp.int32, (tok, tok), 1)
        )
        earlier = jnp.where(earlier, 1.0, 0.0).astype(BF16)
        order = lax.broadcasted_iota(jnp.int32, (cap, tok), 0).astype(F32)

        def one(b, carry):
            named = table_out[b].astype(F32)
            hit = jnp.zeros((1, tok), F32)
            for k in range(top):
                hit = hit + jnp.where(named[k : k + 1] == me.astype(F32), 1.0, 0.0)
            rank = jnp.dot(
                jnp.broadcast_to(hit, (16, tok)).astype(BF16), earlier, preferred_element_type=F32
            )[0:1]
            place = jnp.where(order == rank, 1.0, 0.0) * hit
            rows_out[pl.ds(pl.multiple_of(b * cap, cap), cap), :] = jnp.dot(
                place.astype(BF16), rows_in[b], preferred_element_type=F32
            ).astype(BF16)
            return carry

        lax.fori_loop(0, n, one, 0)

    def send_own(a):
        for way in (1, 2, 0):
            guarded(ways[way][1], lambda a=a, way=way: copy(a, me, None, way).start())

    def pass_on(a):
        for hop, slot, here, way in hops:

            def relay(a=a, hop=hop, slot=slot, way=way):
                copy(a, slot, hop, way).wait_recv()
                pl.when(ways[way][1])(lambda: copy(a, slot, hop, way).start())
                copy(a, slot, hop, 0).start()

            pl.when(here)(relay)

    def finish(a):
        for chip in range(chips):
            copy(a, 2 * chip + 1 - core, 0, 0).wait_recv()

    send_own(0)
    send_own(1)
    pass_on(0)
    pass_on(1)
    send_own(2)
    for c in locals_():
        c.wait()
    finish(0)
    finish(1)
    load_w.wait()
    tile = 256
    steps = proj.shape[1] // tile
    width = steps // len(hops) if steps >= len(hops) else 0

    def columns(first, last):
        def one(i, carry):
            at = pl.ds(pl.multiple_of(i * tile, tile), tile)
            proj[:, at] = jnp.dot(rows_x[...], w_vmem[:, at], preferred_element_type=F32)
            return carry

        lax.fori_loop(first, last, one, 0)

    pick(all_x, rows_x)
    for i, (hop, slot, here, way) in enumerate(hops):

        def relay(hop=hop, slot=slot, way=way):
            copy(2, slot, hop, way).wait_recv()
            pl.when(ways[way][1])(lambda: copy(2, slot, hop, way).start())
            copy(2, slot, hop, 0).start()

        pl.when(here)(relay)
        columns(i * width, (i + 1) * width if i < len(hops) - 1 else steps)
    finish(2)
    pick(all_dy, rows_dy)
    for a in range(count):
        for way in range(3):
            guarded(ways[way][1], lambda a=a, way=way: copy(a, me, None, way).wait_send())
        for hop, slot, here, way in hops:

            def drain(a=a, hop=hop, slot=slot, way=way):
                pl.when(ways[way][1])(lambda: copy(a, slot, hop, way).wait_send())
                copy(a, slot, hop, 0).wait_send()

            pl.when(here)(drain)


def gather_all(n, cap, top, w_one, *arrays):
    table, rows = arrays[:2]
    vmem, width = pl.BlockSpec(memory_space=pltpu.VMEM), rows.shape[1]
    return pl.pallas_call(
        lambda *refs: gather_kernel(n, cap, top, *refs),
        out_shape=[
            jax.ShapeDtypeStruct((n,) + table.shape, BF16),
            jax.ShapeDtypeStruct((n * cap, width), BF16),
            jax.ShapeDtypeStruct((n * cap, width), BF16),
            jax.ShapeDtypeStruct((n * cap, w_one.shape[1]), F32),
        ],
        in_specs=[vmem] * 3 + [pl.BlockSpec(memory_space=pl.ANY)],
        out_specs=[vmem] * 4,
        scratch_shapes=[
            pltpu.VMEM((n,) + rows.shape, BF16),
            pltpu.VMEM((n,) + rows.shape, BF16),
            pltpu.VMEM(w_one.shape, BF16),
            pltpu.SemaphoreType.DMA,
            pltpu.SemaphoreType.DMA((3,)),
            pltpu.SemaphoreType.DMA((3, n - 1, 3)),
            pltpu.SemaphoreType.DMA((3, n)),
        ],
        compiler_params=pltpu.CompilerParams(
            collective_id=0, has_side_effects=True, vmem_limit_bytes=48 * 1024 * 1024
        ),
    )(*arrays, w_one)


def exclusive_rank(hits):
    rows = hits.shape[1]
    earlier = (jnp.arange(rows)[:, None] < jnp.arange(rows)[None, :]).astype(BF16)
    return jnp.dot(hits.astype(BF16), earlier, preferred_element_type=F32)


def dispatch_gather(tokens, out_grad, routes, probs, w_one, cap):
    tok_rows, width = tokens.shape
    top = routes.shape[1]
    me = lax.axis_index("expert").astype(F32)
    table = jnp.concatenate([routes.T.astype(BF16), probs.T], axis=0)
    table = jnp.pad(table, ((0, -2 * top % 16), (0, 0)))
    table, rows_x, rows_dy, proj = gather_all(
        lax.axis_size("expert"), cap, top, w_one, table, tokens, out_grad
    )
    table = table.astype(F32)
    mine = table[:, :top] == me
    hits = jnp.any(mine, axis=1)
    prob = jnp.sum(jnp.where(mine, table[:, top : 2 * top], 0.0), axis=1)
    rank = exclusive_rank(hits)
    place = (rank[:, None, :] == jnp.arange(cap, dtype=F32)[None, :, None]) & hits[:, None, :]
    rows_p = jnp.sum(jnp.where(place, prob[:, None, :], 0.0), axis=2).reshape(-1)
    return rows_x, rows_dy, rows_p, proj


def dispatch_exchange(tokens, out_grad, probs, slot, experts, cap):
    tok_rows, width = tokens.shape
    top = slot.shape[1]
    flat = slot.reshape(-1)
    slot_hit = flat[:, None] == jnp.arange(experts * cap, dtype=jnp.int32)[None, :]
    filled = jnp.any(slot_hit, axis=0)
    owner = jnp.sum(jnp.where(slot_hit, jnp.arange(flat.shape[0], dtype=jnp.int32)[:, None], 0), axis=0)
    source = owner // top
    zero = jnp.zeros((), BF16)

    def move(rows):
        return lax.all_to_all(rows, "expert", split_axis=0, concat_axis=0, tiled=True)

    send_x = jnp.where(filled[:, None], tokens[source], zero).reshape(experts, cap, width)
    send_dy = jnp.where(filled[:, None], out_grad[source], zero).reshape(experts, cap, width)
    send_p = jnp.where(filled, probs.reshape(-1)[owner], zero).reshape(experts, cap)
    return (
        move(send_x).reshape(-1, width),
        move(send_dy).reshape(-1, width),
        move(send_p).reshape(-1).astype(F32),
    )


def fused_kernel(top, *refs):
    routes_hbm, probs_hbm, x_hbm, dy_hbm, w1_hbm, w2_hbm = refs[:6]
    outputs = refs[6:10]
    tabs, all_x, all_dy, w1, w2, rows_x, rows_dy, places, chance = refs[10:19]
    slope_up, act_keep, hid_keep, hid_t, pg, xs, xs_t, g1_sum = refs[19:27]
    ret, ret_p, got, got_p, own_t, part_s, part_r = refs[27:34]
    own_sem, w_sem, z_send, z_recv, xs_send, xs_recv, pg_send, pg_recv = refs[34:42]
    fw_send, fw_recv, ret_send, ret_recv, part_send, part_recv, keep_sem = refs[42:49]
    back_sum, tok_out, prob_out, g1_out, g2_out, out_sem, g1_sem, routes_in, probs_in, named_sem = refs[49:]
    count = 6
    n, tok, width = all_x.shape
    rows = rows_x.shape[1]
    cap = rows // 2
    hidden = w2.shape[0]
    share = width // 4
    half_hidden = hidden // 2
    chips = n // 2
    me, rep = lax.axis_index("expert"), lax.axis_index("dp")
    z, core = me // 2, me % 2
    rep_x = rep + 1 - 2 * (rep % 2)
    rep_y = rep + 2 - 4 * (rep // 2)
    rep_d = 3 - rep
    tile = 256

    barrier = pltpu.get_barrier_semaphore()
    for i in range(1, n):
        pl.semaphore_signal(
            barrier, inc=1, device_id={"expert": (me + i) % n}, device_id_type=pl.DeviceIdType.MESH
        )
    for target in (rep_x, rep_y, rep_d):
        pl.semaphore_signal(
            barrier, inc=1, device_id={"dp": target}, device_id_type=pl.DeviceIdType.MESH
        )

    columns = (rep_d, rep_x, rep_y, rep)

    def quarter(i):
        return pl.ds(pl.multiple_of(columns[i] * share, share), share)

    def own(a):
        return (tabs.at[me], x_hbm)[a] if a < 2 else dy_hbm.at[:, quarter(a - 2)]

    def held(a, slot):
        return (tabs, all_x)[a].at[slot] if a < 2 else all_dy.at[slot, :, quarter(a - 2)]

    loads = [pltpu.make_async_copy(w1_hbm, w1, w_sem.at[0]), pltpu.make_async_copy(w2_hbm, w2, w_sem.at[1])]
    keeps = [
        pltpu.make_async_copy(x_hbm, all_x.at[me], own_sem.at[0]),
        pltpu.make_async_copy(dy_hbm, all_dy.at[me], own_sem.at[1]),
    ]
    names = [
        pltpu.make_async_copy(routes_hbm, routes_in, named_sem.at[0]),
        pltpu.make_async_copy(probs_hbm, probs_in, named_sem.at[1]),
    ]
    for c in names + keeps + loads:
        c.start()
    for c in names:
        c.wait()
    tabs[me] = jnp.concatenate(
        [routes_in[...].astype(F32), probs_in[...].astype(F32), jnp.zeros((16 - 2 * top, tok), F32)], axis=0
    ).astype(BF16)

    pl.semaphore_wait(barrier, n - 1 + 3)

    ways = ((me - core + 1 - core, None), (me + 2, z < chips - 1), (me - 2, z > 0))

    def guarded(ok, body):
        if ok is None:
            body()
        else:
            pl.when(ok)(body)

    def send(src, dst, send_sem, recv_sem, device):
        return pltpu.make_async_remote_copy(
            src_ref=src,
            dst_ref=dst,
            send_sem=send_sem,
            recv_sem=recv_sem,
            device_id=device,
            device_id_type=pl.DeviceIdType.MESH,
        )

    def along(a, slot, hop, way):
        source = own(a) if hop is None else held(a, slot)
        return send(
            source,
            held(a, slot),
            z_send.at[a, 0 if hop is None else hop, way],
            z_recv.at[a, slot],
            {"expert": ways[way][0]},
        )

    def hops(step):
        return (
            (2 * step - 1, me - 2 * step, z - step >= 0, 1),
            (2 * step, me + 2 * step, z + step < chips, 2),
        )

    def pass_on(a, step):
        for hop, slot, here, way in hops(step):

            def relay(hop=hop, slot=slot, way=way):
                along(a, slot, hop, way).wait_recv()
                pl.when(ways[way][1])(lambda: along(a, slot, hop, way).start())
                along(a, slot, hop, 0).start()

            pl.when(here)(relay)

    def chip_of(k):
        upper = z // 2
        low = z + upper * (3 - 2 * z)
        near = k + low * (1 - k // 2) * (1 - 2 * k)
        return near + upper * (3 - 2 * near)

    def slice_copy(k, i):
        target = (rep_x, rep_y, rep_d)[i]
        return send(
            rows_x.at[k, :, pl.ds(pl.multiple_of(target * share, share), share)],
            xs.at[k * 4 + rep],
            xs_send.at[k, i],
            xs_recv.at[k, rep],
            {"dp": target},
        )

    def slice_wait(k, other):
        send(
            rows_x.at[k, :, pl.ds(0, share)], xs.at[k * 4 + other], xs_send.at[k, 0], xs_recv.at[k, other], {"dp": other}
        ).wait_recv()

    def grad_copy(k, i):
        return send(
            pg.at[k * 4 + rep], pg.at[k * 4 + rep], pg_send.at[k, i], pg_recv.at[k, rep], {"dp": (rep_x, rep_y)[i]}
        )

    def grad_wait(k, other):
        send(pg.at[k * 4 + other], pg.at[k * 4 + other], pg_send.at[k, 0], pg_recv.at[k, other], {"dp": other}).wait_recv()

    def forward_copy(k, i):
        came, goes = ((rep_x, rep_y), (rep_y, rep_x))[i]
        part = pg.at[k * 4 + came, pl.ds(i * cap, cap)]
        return send(part, part, fw_send.at[k, i], fw_recv.at[k, i], {"dp": goes})

    def forward_wait(k):
        for i in range(2):
            part = pg.at[k * 4 + rep_d, pl.ds(i * cap, cap)]
            send(part, part, fw_send.at[k, i], fw_recv.at[k, i], {"dp": (rep_y, rep_x)[i]}).wait_recv()

    def forward(k):
        grad_wait(k, rep_x)
        forward_copy(k, 0).start()
        grad_wait(k, rep_y)
        forward_copy(k, 1).start()

    def return_copy(k, i):
        return send(
            ret.at[k, pl.ds(i * cap, cap)],
            got.at[me],
            ret_send.at[k, i],
            ret_recv.at[me],
            {"expert": 2 * chip_of(k) + i},
        )

    def return_prob(k, i):
        return send(
            ret_p.at[k], got_p.at[me], ret_send.at[k, 2 + i], ret_recv.at[n + me], {"expert": 2 * chip_of(k) + i}
        )

    def give_back(k):
        for i in range(2):

            @pl.when(2 * chip_of(k) + i != me)
            def _(i=i):
                return_prob(k, i).start()
                return_copy(k, i).start()

    def keep_own():
        return [
            pltpu.make_async_copy(ret.at[0, pl.ds(core * cap, cap)], got.at[me], keep_sem.at[0]),
            pltpu.make_async_copy(ret_p.at[0], got_p.at[me], keep_sem.at[1]),
        ]

    def piece(column, half):
        dy = rows_dy[:, :, pl.ds(pl.multiple_of(column * share, share), share)].reshape(chips * rows, share)
        return jnp.dot(
            hid_t[half * half_hidden : (half + 1) * half_hidden], dy, preferred_element_type=F32
        )

    sides = (rep_x, rep_y, rep_x, rep_y, rep_y, rep_x)

    def part_copy(i):
        return send(part_s.at[i], part_r.at[i], part_send.at[i], part_recv.at[i], {"dp": sides[i]})

    def first_parts(i):
        for slot in ((0, 1), (2,), (3,), ())[i]:
            part_s[slot] = piece(columns[i], slot % 2).astype(BF16)
            part_copy(slot).start()

    for a in range(count):
        for way in (1, 2, 0):
            guarded(ways[way][1], lambda a=a, way=way: along(a, me, None, way).start())

    earlier = lax.broadcasted_iota(jnp.int32, (tok, tok), 0) < lax.broadcasted_iota(jnp.int32, (tok, tok), 1)
    earlier = jnp.where(earlier, 1.0, 0.0).astype(BF16)
    order = lax.broadcasted_iota(jnp.int32, (cap, tok), 0).astype(F32)

    def placing(named, expert):
        hit = jnp.zeros((1, tok), F32)
        prob = jnp.zeros((1, tok), F32)
        for k in range(top):
            match = jnp.where(named[k : k + 1] == expert, 1.0, 0.0)
            hit = hit + match
            prob = prob + match * named[top + k : top + k + 1]
        rank = jnp.dot(
            jnp.broadcast_to(hit, (16, tok)).astype(BF16), earlier, preferred_element_type=F32
        )[0:1]
        return jnp.where(order == rank, 1.0, 0.0) * hit, prob

    nt = (((1,), (1,)), ((), ()))

    def pick(source, target, k, chip, column):
        at = pl.ds(pl.multiple_of(column * share, share), share)
        pair = source[pl.ds(2 * chip, 2), :, at].reshape(2 * tok, share)
        target[k, :, at] = jnp.dot(places[...], pair, preferred_element_type=F32).astype(BF16)

    def chunk(k, carry):
        chip = chip_of(k)
        other = 2 * chip + 1 - core

        def relays(a):
            pl.when(k > 0)(lambda: pass_on(a, k))
            if a in (1, 2):
                pl.when(k == 0)(keeps[a - 1].wait)
            along(a, other, 0, 0).wait_recv()

        relays(0)
        blocks, probs = [], []
        blank = jnp.zeros((cap, tok), F32)
        for i in range(2):
            place, prob = placing(tabs[2 * chip + i].astype(F32), me.astype(F32))
            blocks.append(jnp.concatenate([blank] * i + [place] + [blank] * (1 - i), axis=1))
            probs.append(jnp.sum(place * prob, axis=1, keepdims=True))
        places[...] = jnp.concatenate(blocks, axis=0).astype(BF16)
        chance[...] = jnp.broadcast_to(jnp.concatenate(probs, axis=0), chance.shape)
        relays(1)
        for i in (2, 0, 1):
            pick(all_x, rows_x, k, chip, (rep_x, rep_y, rep_d)[i])
            slice_copy(k, i).start()
        pick(all_x, rows_x, k, chip, rep)
        xs[k * 4 + rep] = rows_x[k, :, pl.ds(pl.multiple_of(rep * share, share), share)]
        pl.when(k == 0)(loads[0].wait)

        def units(j, carry):
            at = pl.ds(pl.multiple_of(j * tile, tile), tile)
            up_at = pl.ds(pl.multiple_of(hidden + j * tile, tile), tile)
            gate = jnp.dot(rows_x[k], w1[:, at], preferred_element_type=F32)
            upper = jnp.dot(rows_x[k], w1[:, up_at], preferred_element_type=F32)
            sig = jax.nn.sigmoid(gate)
            act = gate * sig
            hid = (act * upper).astype(BF16)
            scaled = chance[:, 0:1] * hid.astype(F32)
            slope_up[:, at] = upper * (sig * (1.0 + gate * (1.0 - sig)))
            act_keep[:, at] = act
            hid_keep[:, at] = hid
            hid_t[at, pl.ds(pl.multiple_of(k * rows, rows), rows)] = scaled.T.astype(BF16)
            return carry

        lax.fori_loop(0, hidden // tile, units, 0)
        pl.when(k > 0)(lambda: forward(k - 1))
        for i in range(4):
            relays(2 + i)
            pick(all_dy, rows_dy, k, chip, columns[i])
            pl.when(k == chips - 1)(lambda i=i: first_parts(i))
            if i == 0:
                pl.when(k == 0)(loads[1].wait)
            gained = lax.dot_general(
                rows_dy[k, :, quarter(i)], w2[:, quarter(i)], nt, preferred_element_type=F32
            )
            back_sum[...] = gained if i == 0 else back_sum[...] + gained

        def backs(j, total):
            at = pl.ds(pl.multiple_of(j * tile, tile), tile)
            up_at = pl.ds(pl.multiple_of(hidden + j * tile, tile), tile)
            back = back_sum[:, at]
            hid_grad = chance[:, 0:1] * back
            pg[k * 4 + rep, :, at] = (hid_grad * slope_up[:, at]).astype(BF16)
            pg[k * 4 + rep, :, up_at] = (hid_grad * act_keep[:, at]).astype(BF16)
            return total + jnp.sum(back * hid_keep[:, at].astype(F32), axis=1, keepdims=True)

        dprob = lax.fori_loop(0, hidden // tile, backs, jnp.zeros((rows, 1), F32))
        ret_p[k] = jnp.broadcast_to(dprob, (rows, 128)).T[0:16].astype(BF16)
        for i in range(2):
            grad_copy(k, i).start()

        def rows_back(j, carry):
            at = pl.ds(pl.multiple_of(j * tile, tile), tile)
            ret[k, :, at] = lax.dot_general(
                pg[k * 4 + rep], w1[at, :], nt, preferred_element_type=F32
            ).astype(BF16)
            return carry

        lax.fori_loop(0, width // tile, rows_back, 0)

        @pl.when(k == 0)
        def _():
            give_back(0)
            for c in keep_own():
                c.start()

        @pl.when(k == 2)
        def _():
            give_back(1)
            give_back(2)

        pl.when(k == 3)(lambda: give_back(3))
        return carry

    lax.fori_loop(0, chips, chunk, 0)

    origin = (rep, rep_x, rep_y, rep_d)

    def turn(k):
        for p in range(4):
            if p:
                slice_wait(k, origin[p])
            at = k * 4 + p
            xs_t[:, at * rows : (at + 1) * rows] = xs[k * 4 + origin[p]].astype(F32).T.astype(BF16)

    def gathered(k, at, first, last):
        return [pg[k * 4 + origin[p], :, at] for p in range(first, last)]

    early = 4 * (chips - 1)
    for k in range(chips - 1):
        turn(k)
        forward_wait(k)

    def sums(j, carry):
        at = pl.ds(pl.multiple_of(j * tile, tile), tile)
        parts = [part for k in range(chips - 1) for part in gathered(k, at, 0, 4)]
        g1_sum[:, at] = jnp.dot(
            xs_t[:, : early * rows], jnp.concatenate(parts, axis=0), preferred_element_type=F32
        )
        return carry

    lax.fori_loop(0, 2 * hidden // tile, sums, 0)
    for half in range(2):
        part_copy(half).wait_recv()
        mine = piece((rep_y, rep_x)[half], half)
        part_s[4 + half] = (mine + part_r[half].astype(F32)).astype(BF16)
        part_copy(4 + half).start()
    turn(chips - 1)

    named = tabs[me].astype(F32)
    owns = [placing(named, float(e))[0] for e in range(n)]
    for c in range(chips):
        own_t[:, c * 2 * cap : (c + 1) * 2 * cap] = (
            jnp.concatenate([owns[2 * c], owns[2 * c + 1]], axis=0).T.astype(BF16)
        )
    forward(chips - 1)

    def near(j, carry):
        at = pl.ds(pl.multiple_of(j * tile, tile), tile)
        g1_sum[:, at] = g1_sum[:, at] + jnp.dot(
            xs_t[:, early * rows : (early + 3) * rows],
            jnp.concatenate(gathered(chips - 1, at, 0, 3), axis=0),
            preferred_element_type=F32,
        )
        return carry

    lax.fori_loop(0, 2 * hidden // tile, near, 0)
    writes = [
        pltpu.make_async_copy(ref, outputs[i], out_sem.at[i])
        for i, ref in ((0, tok_out), (1, prob_out), (3, g2_out))
    ]
    for half in range(2):
        mine = piece(rep, half)
        part_copy(2 + half).wait_recv()
        part_copy(4 + half).wait_recv()
        g2_out[half * half_hidden : (half + 1) * half_hidden, :] = (
            mine + part_r[2 + half].astype(F32) + part_r[4 + half].astype(F32)
        ).astype(BF16)
    writes[2].start()

    for c in keep_own():
        c.wait()
    for e in range(n):

        @pl.when(e != me)
        def _(e=e):
            here = {"expert": e}
            send(ret_p.at[0], got_p.at[e], ret_send.at[0, 2], ret_recv.at[n + e], here).wait_recv()
            send(ret.at[0, pl.ds(0, cap)], got.at[e], ret_send.at[0, 0], ret_recv.at[e], here).wait_recv()

    def combine(j, carry):
        at = pl.ds(pl.multiple_of(j * tile, tile), tile)
        tok_out[:, at] = jnp.dot(
            own_t[...], got[:, :, at].reshape(n * cap, tile), preferred_element_type=F32
        ).astype(BF16)
        return carry

    lax.fori_loop(0, width // tile, combine, 0)
    writes[0].start()
    found = [jnp.zeros((1, tok), F32)] * top
    odd = core.astype(F32)
    for e in range(n):
        spot = jnp.concatenate([owns[e] * (1.0 - odd), owns[e] * odd], axis=0).astype(BF16)
        value = jnp.dot(got_p[e], spot, preferred_element_type=F32)[0:1]
        found = [found[k] + jnp.where(named[k : k + 1] == float(e), value, 0.0) for k in range(top)]
    prob_out[...] = jnp.concatenate(found, axis=0).astype(BF16)
    writes[1].start()
    forward_wait(chips - 1)

    def put(j):
        at = pl.ds(pl.multiple_of(j * tile, tile), tile)
        return pltpu.make_async_copy(g1_out.at[:, at], outputs[2].at[:, at], g1_sem.at[j])

    def finals(j, carry):
        at = pl.ds(pl.multiple_of(j * tile, tile), tile)
        g1_out[:, at] = (
            g1_sum[:, at]
            + jnp.dot(xs_t[:, (early + 3) * rows :], pg[early + rep_d, :, at], preferred_element_type=F32)
        ).astype(BF16)
        put(j).start()
        return carry

    lax.fori_loop(0, 2 * hidden // tile, finals, 0)

    for a in range(count):
        for way in range(3):
            guarded(ways[way][1], lambda a=a, way=way: along(a, me, None, way).wait_send())

    def drain(step, carry):
        for a in range(count):
            for hop, slot, here, way in hops(step):

                def one(a=a, hop=hop, slot=slot, way=way):
                    pl.when(ways[way][1])(lambda: along(a, slot, hop, way).wait_send())
                    along(a, slot, hop, 0).wait_send()

                pl.when(here)(one)
        return carry

    lax.fori_loop(1, chips, drain, 0)

    def drain_chunk(k, carry):
        for i in range(3):
            slice_copy(k, i).wait_send()
        for i in range(2):
            grad_copy(k, i).wait_send()
            forward_copy(k, i).wait_send()

            @pl.when(2 * chip_of(k) + i != me)
            def _(i=i):
                return_prob(k, i).wait_send()
                return_copy(k, i).wait_send()

        return carry

    lax.fori_loop(0, chips, drain_chunk, 0)
    for i in range(6):
        part_copy(i).wait_send()
    for c in writes:
        c.wait()
    for j in range(2 * hidden // tile):
        put(j).wait()


def settle_kernel(blocks, *refs):
    count = len(refs) // 3
    ins, outs, held, sem = refs[:count], refs[count : 2 * count], refs[2 * count : 3 * count], refs[-1]
    takes, gives = [], []
    for i in range(count):
        cuts = blocks if ins[i].shape[0] % (16 * blocks) == 0 else 1
        size = ins[i].shape[0] // cuts
        for j in range(cuts):
            at = pl.ds(j * size, size)
            takes.append(pltpu.make_async_copy(ins[i].at[at], held[i].at[at], sem.at[0, i, j]))
            gives.append(pltpu.make_async_copy(held[i].at[at], outs[i].at[at], sem.at[1, i, j]))
    for c in takes:
        c.start()
    for take, give in zip(takes, gives):
        take.wait()
        give.start()
    for c in gives:
        c.wait()


def settle(arrays):
    count = len(arrays)
    return pl.pallas_call(
        lambda *refs: settle_kernel(4, *refs),
        out_shape=[jax.ShapeDtypeStruct(a.shape, a.dtype) for a in arrays],
        in_specs=[pl.BlockSpec(memory_space=pl.ANY)] * count,
        out_specs=[pl.BlockSpec(memory_space=pl.ANY)] * count,
        scratch_shapes=[pltpu.VMEM(a.shape, a.dtype) for a in arrays] + [pltpu.SemaphoreType.DMA((2, count, 4))],
        compiler_params=pltpu.CompilerParams(vmem_limit_bytes=62 * 1024 * 1024),
    )(*arrays)


def fused(tokens, out_grad, routes, probs, w_one, w_two, n, cap):
    tok, width = tokens.shape
    top, hidden = routes.shape[1], w_two.shape[0]
    chips, rows, share = n // 2, 2 * cap, width // 4
    hbm = pl.BlockSpec(memory_space=pl.ANY)
    dma = pltpu.SemaphoreType.DMA
    results = pl.pallas_call(
        lambda *refs: fused_kernel(top, *refs),
        out_shape=[
            jax.ShapeDtypeStruct((tok, width), BF16),
            jax.ShapeDtypeStruct((top, tok), BF16),
            jax.ShapeDtypeStruct((share, 2 * hidden), BF16),
            jax.ShapeDtypeStruct((hidden, share), BF16),
        ],
        in_specs=[hbm] * 6,
        out_specs=[hbm] * 4,
        scratch_shapes=[
            pltpu.VMEM((n, 16, tok), BF16),
            pltpu.VMEM((n, tok, width), BF16),
            pltpu.VMEM((n, tok, width), BF16),
            pltpu.VMEM((width, 2 * hidden), BF16),
            pltpu.VMEM((hidden, width), BF16),
            pltpu.VMEM((chips, rows, width), BF16),
            pltpu.VMEM((chips, rows, width), BF16),
            pltpu.VMEM((rows, 2 * tok), BF16),
            pltpu.VMEM((rows, 128), F32),
            pltpu.VMEM((rows, hidden), F32),
            pltpu.VMEM((rows, hidden), F32),
            pltpu.VMEM((rows, hidden), BF16),
            pltpu.VMEM((hidden, chips * rows), BF16),
            pltpu.VMEM((chips * 4, rows, 2 * hidden), BF16),
            pltpu.VMEM((chips * 4, rows, share), BF16),
            pltpu.VMEM((share, chips * 4 * rows), BF16),
            pltpu.VMEM((share, 2 * hidden), F32),
            pltpu.VMEM((chips, rows, width), BF16),
            pltpu.VMEM((chips, 16, rows), BF16),
            pltpu.VMEM((n, cap, width), BF16),
            pltpu.VMEM((n, 16, rows), BF16),
            pltpu.VMEM((tok, n * cap), BF16),
            pltpu.VMEM((6, hidden // 2, share), BF16),
            pltpu.VMEM((6, hidden // 2, share), BF16),
            dma((2,)),
            dma((2,)),
            dma((6, n - 1, 3)),
            dma((6, n)),
            dma((chips, 3)),
            dma((chips, 4)),
            dma((chips, 2)),
            dma((chips, 4)),
            dma((chips, 2)),
            dma((chips, 2)),
            dma((chips, 4)),
            dma((2 * n,)),
            dma((6,)),
            dma((6,)),
            dma((2,)),
            pltpu.VMEM((rows, hidden), F32),
            pltpu.VMEM((tok, width), BF16),
            pltpu.VMEM((top, tok), BF16),
            pltpu.VMEM((share, 2 * hidden), BF16),
            pltpu.VMEM((hidden, share), BF16),
            dma((4,)),
            dma((2 * hidden // 256,)),
            pltpu.VMEM((top, tok), jnp.int32),
            pltpu.VMEM((top, tok), BF16),
            dma((2,)),
        ],
        compiler_params=pltpu.CompilerParams(
            collective_id=0, has_side_effects=True, vmem_limit_bytes=62 * 1024 * 1024
        ),
    )(routes.T, probs.T, tokens, out_grad, w_one, w_two)
    token_grad, prob, share_one, share_two = settle(results)
    return token_grad, prob.T, share_one[None], share_two[None]


def swap(value, flip):
    return lax.ppermute(value, "dp", [(i, i ^ flip) for i in range(4)])


def square_first(piece):
    got = []
    for rest in (True, False):
        for half, side in ((0, 1), (1, 2)):
            flip = 3 if rest else side
            got.append(swap(piece(flip, half).astype(BF16), side))
    return got


def square_second(piece, got):
    sent = []
    for half, side in ((0, 2), (1, 1)):
        total = (piece(side, half) + got[half].astype(F32)).astype(BF16)
        sent.append(swap(total, side))
    return [
        (piece(0, half) + got[2 + half].astype(F32) + sent[half].astype(F32)).astype(BF16)
        for half in range(2)
    ]


def shards(tokens, out_grad, routes, probs, w_in, w_out):
    tok_rows, width = tokens.shape
    top = routes.shape[1]
    n_groups = lax.axis_size("expert")
    experts = n_groups * w_in.shape[0]
    hidden = w_out.shape[1]
    cap = 4 * tok_rows * top // (3 * experts)
    w_one, w_two = w_in[0], w_out[0]
    if n_groups == 8 and lax.axis_size("dp") == 4:
        return fused(tokens, out_grad, routes, probs, w_one, w_two, n_groups, cap)

    names = jnp.arange(experts, dtype=jnp.int32)
    named = routes[:, :, None] == names[None, None, :]
    hits = jnp.any(named, axis=1)
    later = (jnp.arange(tok_rows)[:, None] > jnp.arange(tok_rows)[None, :]).astype(BF16)
    rank = jnp.dot(later, hits.astype(BF16), preferred_element_type=F32)
    own_rank = jnp.sum(jnp.where(named, rank[:, None, :], 0.0), axis=2).astype(jnp.int32)
    slot = routes * cap + own_rank

    if experts <= 16:
        rows_x, rows_dy, rows_p, proj = dispatch_gather(tokens, out_grad, routes, probs, w_one, cap)
    else:
        rows_x, rows_dy, rows_p = dispatch_exchange(tokens, out_grad, probs, slot, experts, cap)
        proj = jnp.dot(rows_x, w_one, preferred_element_type=F32)
    rows_p = rows_p[:, None]
    gate, upper = proj[:, :hidden], proj[:, hidden:]
    sig = jax.nn.sigmoid(gate)
    act = gate * sig
    hid = (act * upper).astype(BF16)
    scaled = (rows_p * hid.astype(F32)).astype(BF16)
    replicas = lax.axis_size("dp")
    part = width // replicas
    at = lax.axis_index("dp")
    contract = (((0,), (0,)), ((), ()))

    def piece_two(flip, half):
        cut = lax.dynamic_slice_in_dim(rows_dy, (at ^ flip) * part, part, axis=1)
        units = scaled[:, half * (hidden // 2) : (half + 1) * (hidden // 2)]
        return lax.dot_general(units, cut, contract, preferred_element_type=F32)

    if replicas == 4:
        first_two = square_first(piece_two)
    else:
        grad_two = lax.dot_general(scaled, rows_dy, contract, preferred_element_type=F32).astype(BF16)
        share_two = lax.psum_scatter(grad_two, "dp", scatter_dimension=1, tiled=True)

    back = lax.dot_general(rows_dy, w_two, (((1,), (1,)), ((), ())), preferred_element_type=F32)
    dprob = jnp.sum(back * hid.astype(F32), axis=1).astype(BF16)
    hid_grad = rows_p * back
    proj_grad = jnp.concatenate(
        [hid_grad * upper * (sig * (1.0 + gate * (1.0 - sig))), hid_grad * act], axis=1
    ).astype(BF16)

    def piece_one(flip, half):
        cut = lax.dynamic_slice_in_dim(rows_x, (at ^ flip) * part, part, axis=1)
        units = proj_grad[:, half * hidden : (half + 1) * hidden]
        return lax.dot_general(cut, units, contract, preferred_element_type=F32)

    if replicas == 4:
        first_one = square_first(piece_one)
        second_two = square_second(piece_two, first_two)
        second_one = square_second(piece_one, first_one)
        share_two = jnp.concatenate(second_two, axis=0)
        share_one = jnp.concatenate(second_one, axis=1)
    else:
        grad_one = lax.dot_general(rows_x, proj_grad, contract, preferred_element_type=F32).astype(BF16)
        share_one = lax.psum_scatter(grad_one, "dp", scatter_dimension=0, tiled=True)

    row_grad = lax.dot_general(
        proj_grad, w_one, (((1,), (1,)), ((), ())), preferred_element_type=F32
    ).astype(BF16)
    back_x = lax.all_to_all(
        row_grad.reshape(n_groups, cap, width), "expert", split_axis=0, concat_axis=0, tiled=True
    ).reshape(experts * cap, width)
    back_p = lax.all_to_all(
        dprob.reshape(n_groups, cap), "expert", split_axis=0, concat_axis=0, tiled=True
    ).reshape(-1)
    slots = jnp.arange(experts * cap, dtype=jnp.int32)
    held = slot[:, :, None] == slots[None, None, :]
    prob_grad = jnp.sum(jnp.where(held, back_p.astype(F32), 0.0), axis=2).astype(BF16)
    token_grad = jnp.dot(
        jnp.any(held, axis=1).astype(BF16), back_x, preferred_element_type=F32
    ).astype(BF16)
    return token_grad, prob_grad, share_one[None], share_two[None]


def solution(mesh):
    return jax.shard_map(
        shards,
        mesh=mesh,
        in_specs=(
            P(("dp", "expert"), None),
            P(("dp", "expert"), None),
            P(("dp", "expert"), None),
            P(("dp", "expert"), None),
            P("expert", None, None),
            P("expert", None, None),
        ),
        out_specs=(
            P(("dp", "expert"), None),
            P(("dp", "expert"), None),
            P("expert", "dp", None),
            P("expert", None, "dp"),
        ),
        check_vma=False,
    )
```
